256 devices in a mesh: grp: 16 (over z, core), ing: 16 (over y, x).
Axes of the slice: x: 4, y: 4, z: 8, core: 2. Of those that a mesh axis runs over, the one named last changes fastest.
Arguments:
- amplitudes: bfloat16 [512, 800, 800], P('grp', 'ing'), may hold values from -6 to 6
- integrals: bfloat16 [512, 800, 800], P('grp', 'ing'), may hold values from -0.0024414062 to 0.0024414062
- fock_block: bfloat16 [800, 800], P('ing'), may hold values from -0.625 to 0.625
- virtual_irrep: int32 [800], replicated, may hold values from 0 to 7, as said below
- pair_irrep: int32 [512], P(('grp', 'ing')), may hold values from 0 to 7
- pair_energy: float32 [512], P(('grp', 'ing')), may hold values from -4 to -1
- virtual_energy: float32 [800], replicated, may hold values from 0.5 to 4
Outputs:
- update: float32 [512, 800, 800], P('grp', 'ing')
The draws below stay inside these ranges and needn't reach their ends.
Inputs may be any that keep to these rules, and one draw needn't show every extreme that they name: `virtual_irrep`: the orbitals of one irreducible representation form one contiguous run of 100 plus or minus at most 25 orbitals, and all 8 representations occur.
All inputs are finite; a program needn't handle non-finite values.
Results may differ from the reference program's by a relative error of at most 0.0029.
Values may be sent and summed in bfloat16 or wider, within the bound.
A program may use at most 128 MiB of HBM per device.

```python
import jax
import jax.numpy as jnp
from jax import lax

NV = 800
PAIRS = 512


def draw_virtual_irrep(key, part):
    centre_size = NV // 8
    deviation = jax.random.randint(jax.random.fold_in(key, 11), (4,), 0, NV // 32 + 1)
    run_lengths = jnp.stack([centre_size + deviation, centre_size - deviation], axis=1).reshape(8)
    run_ends = jnp.cumsum(run_lengths)
    position = jnp.arange(NV)
    label_block = jnp.sum((position[:, None] >= run_ends[None, :7]).astype(jnp.int32), axis=1)
    irrep_order = jax.random.permutation(jax.random.fold_in(key, 12), 8)
    return irrep_order[label_block].astype(jnp.int32)


def with_ends(result, own_key, smallest, top_value):
    longest = result.shape.index(max(result.shape))
    spots = []
    for shift in (0, 1):
        where = [jax.random.randint(jax.random.fold_in(own_key, axis), (), 0, length) for axis, length in enumerate(result.shape)]
        where[longest] = (where[longest] + shift) % result.shape[longest]
        spots.append(tuple(where))
    return result.at[spots[0]].set(smallest).at[spots[1]].set(top_value)


def shard_levels(own_key, shape, shards, smallest, top_value):
    factor_of, own = 1.0, jax.random.fold_in(own_key, 6)
    for axis_at, shards_of in shards:
        steps = jnp.exp(jax.random.uniform(jax.random.fold_in(own, axis_at), (shards_of,), jnp.float32, smallest / len(shards), top_value / len(shards)))
        factor_of = factor_of * jnp.repeat(steps, shape[axis_at] // shards_of).reshape([-1 if axis == axis_at else 1 for axis in range(len(shape))])
    return factor_of


def scatter_about(rng, shape, scale, bound, shards=(), dtype=jnp.bfloat16):
    loudness = shard_levels(rng, shape, shards, -0.22, 0.18) if shards else 1.0
    array = jax.random.normal(rng, shape, jnp.float32) * scale * loudness
    return jnp.minimum(jnp.maximum(array, -bound), bound).astype(dtype)


def setup_inputs(seed: int = 0) -> dict:
    key_of = jax.random.split(jax.random.key(seed), 8)
    amplitudes = scatter_about(key_of[0], (PAIRS, NV, NV), 1.0, 6.0, ((0, 16), (1, 16)))
    integrals = scatter_about(key_of[1], (PAIRS, NV, NV), (PAIRS * NV // 8 * 100) ** -0.5, 0.0024414062, ((0, 16), (1, 16)))
    fock_block = scatter_about(key_of[2], (NV, NV), (NV // 8) ** -0.5, 0.625, ((0, 16),))
    virtual_irrep = draw_virtual_irrep(jax.random.fold_in(key_of[7], 71), 0)
    pair_irrep = with_ends(jax.random.randint(key_of[4], (PAIRS,), 0, 8), jax.random.fold_in(key_of[4], 1), 0, 7).astype(jnp.int32)
    pair_energy = jnp.clip(-4.0 + 3.0 * jax.random.uniform(key_of[5], (PAIRS,), jnp.float32) ** shard_levels(key_of[5], (PAIRS,), ((0, 256),), -0.2, 0.2), -4.0, -1.0)
    virtual_energy = jnp.clip(jax.random.uniform(key_of[6], (NV,), jnp.float32, 0.5, 4.0), 0.5, 4.0)
    return {"amplitudes": amplitudes, "integrals": integrals, "fock_block": fock_block, "virtual_irrep": virtual_irrep, "pair_irrep": pair_irrep, "pair_energy": pair_energy, "virtual_energy": virtual_energy}


def masked(values, pair_irrep, virtual_irrep):
    allowed = jnp.bitwise_xor(virtual_irrep[:, None], virtual_irrep[None, :])[None] == pair_irrep[:, None, None]
    return jnp.where(allowed, values, jnp.zeros_like(values))


def reference(amplitudes, integrals, fock_block, virtual_irrep, pair_irrep, pair_energy, virtual_energy):
    amp_masked = masked(amplitudes, pair_irrep, virtual_irrep)
    int_masked = masked(integrals, pair_irrep, virtual_irrep)

    def accumulate(total, pieces):
        return total + jnp.dot(pieces[0], pieces[1].T, preferred_element_type=jnp.float32), None

    correction, _ = lax.scan(accumulate, jnp.zeros((NV, NV), jnp.float32), (amp_masked, int_masked))
    same_irrep = virtual_irrep[:, None] == virtual_irrep[None, :]
    fock_part = jnp.where(same_irrep, fock_block.astype(jnp.float32), jnp.zeros((NV, NV), jnp.float32))
    operator_vv = (fock_part + correction).astype(jnp.bfloat16)
    operator_t = operator_vv.T

    def per_pair(pieces):
        product = jnp.dot(pieces[0], operator_t, preferred_element_type=jnp.float32)
        denominator = pieces[1] - virtual_energy[:, None] - virtual_energy[None, :]
        return (product - product.T) / denominator

    return lax.map(per_pair, (amp_masked, pair_energy))
```

```python
import functools

import jax
import jax.numpy as jnp
from jax import lax
from jax.experimental import pallas as pl
from jax.experimental.pallas import tpu as pltpu
from jax.sharding import PartitionSpec as P

NV, LANES, TILES = 800, 128, 7
PADDED = LANES * TILES
ROWS, OWN, GROUP_PAIRS = 50, 2, 32
RING, DEPTH, SIDE = 16, 8, 4
PEERS = 2 * RING
SLICE, SLOT = 25, 32
IN_SLOT, OUT_HALF, OUT_SLOT = 208, 56, 112
MESH = pl.DeviceIdType.MESH
F32, BF16, I32 = jnp.float32, jnp.bfloat16, jnp.int32
NT = (((1,), (1,)), ((), ()))


def tile_of(array, t):
    if t < TILES - 1:
        return array[:, LANES * t : LANES * (t + 1)]
    last = array[:, LANES * t : NV]
    pad = jnp.zeros((array.shape[0], PADDED - NV), array.dtype)
    return jnp.concatenate([last, pad], axis=1)


def main_kernel(
    amps, ints, fock, irrep, energy, pair_irrep, pair_energy,
    result, irreps_out, row_key_out,
    amp_in, int_in, col_key, col_energy, row_key, row_energy, own_key,
    g_send, g_recv, stage, pack_send, pack_recv, nat_a, nat_b, lhs, rhs, int_rhs,
    fock_fold, corr, red_send, red_recv, z_send, z_recv, op_send, op_recv, op_nat,
    inverse, scaled, out_stage, out_send, out_recv,
    amp_sem, int_sem, g_ssem, g_rsem, p_ssem, p_rsem, r_ssem, r_rsem,
    z_ssem, z_rsem, o_ssem, o_rsem, t_ssem, t_rsem,
):
    grp, ing = lax.axis_index("grp"), lax.axis_index("ing")
    z, core = grp // 2, grp % 2
    y, x = ing // SIDE, ing % SIDE
    me = ing * 2 + core

    def plane_peer(k):
        return ((y + k // SIDE) % SIDE) * SIDE + (x + k % SIDE) % SIDE

    def far_peer(k):
        return ((y + 2 + k // SIDE) % SIDE) * SIDE + (x + 2 + k % SIDE) % SIDE

    def on_plane(i, c):
        return (z * 2 + c, i)

    def chunk(j):
        place = pl.ds(OWN * j, OWN)
        return (
            pltpu.make_async_copy(amps.at[place], amp_in.at[place], amp_sem.at[j]),
            pltpu.make_async_copy(ints.at[place], int_in.at[place], int_sem.at[j]),
        )

    def load(k, carry):
        for copy in chunk(plane_peer(k)):
            copy.start()
        return carry

    barrier = pltpu.get_barrier_semaphore()

    def greet(k, carry):
        pl.semaphore_signal(
            barrier, inc=1, device_id=on_plane(plane_peer(k // 2), (core + k) % 2), device_id_type=MESH
        )
        return carry

    def greet_z(k, carry):
        pl.semaphore_signal(
            barrier, inc=1, device_id=(((z + k) % DEPTH) * 2 + core, ing), device_id_type=MESH
        )
        return carry

    lax.fori_loop(1, PEERS, greet, 0)
    lax.fori_loop(1, DEPTH, greet_z, 0)
    lax.fori_loop(0, RING, load, 0)

    for q in range(OWN):
        g_send[q : q + 1, :] = jnp.full((1, LANES), pair_irrep[q], I32)
    g_recv[ing] = g_send[...]

    for t in range(TILES):
        if t < TILES - 1:
            col_key[t : t + 1, :] = irrep[:, LANES * t : LANES * (t + 1)]
        else:
            col_key[t : t + 1, :] = jnp.concatenate(
                [irrep[:, LANES * t : NV], jnp.full((1, PADDED - NV), -1, I32)], axis=1
            )
        col_energy[t : t + 1, :] = tile_of(energy[...], t)
    for t in range(TILES):
        place = slice(LANES * t, LANES * (t + 1))
        keys = jnp.broadcast_to(col_key[t : t + 1, :].astype(F32), (LANES, LANES))
        row_key[place, :] = keys.T.astype(I32)
    own_key[...] = row_key[pl.ds(ROWS * ing, OUT_HALF), :]
    row_key_out[...] = own_key[...]

    pl.semaphore_wait(barrier, PEERS - 1 + DEPTH - 1)

    def g_copy(i, slot, c=None):
        return pltpu.make_async_remote_copy(
            src_ref=g_send, dst_ref=g_recv.at[slot], send_sem=g_ssem.at[i], recv_sem=g_rsem.at[slot],
            device_id=on_plane(i, core), device_id_type=MESH,
        )

    def g_start(k, carry):
        g_copy(plane_peer(k), ing).start()
        return carry

    lax.fori_loop(1, RING, g_start, 0)

    def pack_copy(i, slot):
        return pltpu.make_async_remote_copy(
            src_ref=pack_send.at[i], dst_ref=pack_recv.at[slot], send_sem=p_ssem.at[i],
            recv_sem=p_rsem.at[slot], device_id=on_plane(i, core), device_id_type=MESH,
        )

    def fold_chunk(j):
        keys = own_key[0:ROWS, :]
        for q in range(OWN):
            wanted = keys ^ g_recv[j, q : q + 1, :]
            for which, source in ((0, amp_in), (1, int_in)):
                folded = jnp.zeros((ROWS, LANES), F32)
                for t in range(TILES):
                    if t < TILES - 1:
                        part = source[OWN * j + q, :, LANES * t : LANES * (t + 1)].astype(F32)
                    else:
                        part = source[OWN * j + q, :, LANES * t : NV].astype(F32)
                        part = jnp.concatenate([part, jnp.zeros((ROWS, PADDED - NV), F32)], axis=1)
                    folded = jnp.where(wanted == col_key[t : t + 1, :], part, folded)
                first = ROWS * (which * OWN + q)
                stage[first : first + ROWS, :] = folded
        return stage[...].astype(BF16)

    stage[4 * ROWS : IN_SLOT, :] = jnp.zeros((IN_SLOT - 4 * ROWS, LANES), F32)

    def pack_step(k, carry):
        j = plane_peer(k)
        g_copy(ing, j).wait_recv()
        for copy in chunk(j):
            copy.wait()
        pack_send[j] = fold_chunk(j)
        pack_copy(j, ing).start()
        return carry

    lax.fori_loop(1, RING, pack_step, 0)
    for copy in chunk(ing):
        copy.wait()
    pack_recv[ing] = fold_chunk(ing)

    fock_rows = fock[...].astype(F32)
    fock_keys = own_key[0:ROWS, :]
    folded_fock = jnp.zeros((ROWS, LANES), F32)
    for t in range(TILES):
        folded_fock = jnp.where(fock_keys == col_key[t : t + 1, :], tile_of(fock_rows, t), folded_fock)
    fock_fold[...] = jnp.zeros(fock_fold.shape, F32)
    fock_fold[0:ROWS, :] = folded_fock
    for t in range(TILES):
        place = slice(LANES * t, LANES * (t + 1))
        row_energy[place, :] = jnp.broadcast_to(col_energy[t : t + 1, :], (LANES, LANES)).T
    for q in range(OWN):
        for t in range(TILES):
            place = slice(LANES * t, LANES * (t + 1))
            wanted = row_key[place, :] ^ pair_irrep[q]
            other = jnp.zeros((LANES, LANES), F32)
            for u in range(TILES):
                other = jnp.where(wanted == col_key[u : u + 1, :], col_energy[u : u + 1, :], other)
            inverse[q, place, :] = 1.0 / (pair_energy[q] - row_energy[place, :] - other)
    nat_a[:, NV:PADDED, :] = jnp.zeros((OWN, PADDED - NV, LANES), F32)
    nat_b[:, NV:PADDED, :] = jnp.zeros((OWN, PADDED - NV, LANES), F32)
    op_nat[NV:PADDED, :] = jnp.zeros((PADDED - NV, LANES), F32)
    corr[NV:PADDED, :] = jnp.zeros((PADDED - NV, LANES), F32)

    def unpack(j):
        stage[...] = pack_recv[j].astype(F32)
        place = pl.ds(ROWS * j, ROWS)
        for q in range(OWN):
            nat_a[q, place, :] = stage[ROWS * q : ROWS * (q + 1), :]
            nat_b[q, place, :] = stage[ROWS * (OWN + q) : ROWS * (OWN + q + 1), :]

    unpack(ing)

    def unpack_step(k, carry):
        j = plane_peer(RING - k)
        pack_copy(ing, j).wait_recv()
        unpack(j)
        return carry

    lax.fori_loop(1, RING, unpack_step, 0)

    for q in range(OWN):
        lhs[:, LANES * q : LANES * (q + 1)] = nat_a[q].astype(BF16)
        int_rhs[:, LANES * q : LANES * (q + 1)] = nat_b[q].astype(BF16)
    for r in range(TILES):
        place = slice(LANES * r, LANES * (r + 1))
        low, high = max(r - 1, 0), min(r + 2, TILES)
        block = lax.dot_general(
            lhs[place, :], int_rhs[LANES * low : LANES * high, :], NT, preferred_element_type=F32
        )
        keys = row_key[place, :]
        folded = jnp.zeros((LANES, LANES), F32)
        for t in range(low, high):
            part = block[:, LANES * (t - low) : LANES * (t - low + 1)]
            folded = jnp.where(keys == col_key[t : t + 1, :], part, folded)
        corr[place, :] = folded

    def red_copy(i, c, slot):
        w = i * 2 + c
        return pltpu.make_async_remote_copy(
            src_ref=red_send.at[w], dst_ref=red_recv.at[slot], send_sem=r_ssem.at[w],
            recv_sem=r_rsem.at[slot], device_id=on_plane(i, c), device_id_type=MESH,
        )

    def red_step(k, carry):
        for c in range(2):
            i = far_peer(k)
            w = i * 2 + c
            rows = corr[pl.ds(SLICE * w, SLOT), :]

            @pl.when(w != me)
            def _():
                red_send[w] = rows
                red_copy(i, c, me).start()

            @pl.when(w == me)
            def _():
                red_recv[w] = rows

        return carry

    lax.fori_loop(0, RING, red_step, 0)

    for q in range(OWN):
        rhs[q, :, LANES : 2 * LANES] = (-nat_a[q]).astype(BF16)

    def red_wait(k, carry):
        i, c = plane_peer(k // 2), (core + k) % 2
        red_copy(ing, core, i * 2 + c).wait_recv()
        return carry

    lax.fori_loop(1, PEERS, red_wait, 0)
    total = red_recv[0]
    for w in range(1, PEERS):
        total = total + red_recv[w]
    z_send[...] = total

    def z_copy(dest, slot):
        return pltpu.make_async_remote_copy(
            src_ref=z_send, dst_ref=z_recv.at[slot], send_sem=z_ssem.at[dest],
            recv_sem=z_rsem.at[slot], device_id=(dest * 2 + core, ing), device_id_type=MESH,
        )

    def z_start(k, carry):
        z_copy((z + 3 + k) % DEPTH, z).start()
        return carry

    lax.fori_loop(1, 5, z_start, 0)
    lax.fori_loop(6, 9, z_start, 0)
    z_recv[z] = total

    def z_wait(k, carry):
        z_copy(z, (z + k) % DEPTH).wait_recv()
        return carry

    lax.fori_loop(1, DEPTH, z_wait, 0)
    total = z_recv[0]
    for k in range(1, DEPTH):
        total = total + z_recv[k]
    rows = (fock_fold[pl.ds(SLICE * core, SLOT), :] + total).astype(BF16)
    op_send[...] = rows
    op_recv[me] = rows

    def op_copy(i, c, slot):
        w = i * 2 + c
        return pltpu.make_async_remote_copy(
            src_ref=op_send, dst_ref=op_recv.at[slot], send_sem=o_ssem.at[w],
            recv_sem=o_rsem.at[slot], device_id=on_plane(i, c), device_id_type=MESH,
        )

    def op_start(k, carry):
        for c in range(2):
            i = far_peer(k)

            @pl.when(i * 2 + c != me)
            def _():
                op_copy(i, c, me).start()

        return carry

    lax.fori_loop(0, RING, op_start, 0)

    def op_place(w):
        op_nat[pl.ds(SLICE * w, SLICE), :] = op_recv[w].astype(F32)[0:SLICE, :]

    op_place(me)

    def op_wait(k, carry):
        w = plane_peer(k // 2) * 2 + (core + k) % 2
        op_copy(ing, core, w).wait_recv()
        op_place(w)
        return carry

    lax.fori_loop(1, PEERS, op_wait, 0)

    operator = op_nat[...].astype(BF16)
    for q in range(OWN):
        rhs[q, :, 0:LANES] = operator
        left = jnp.concatenate([lhs[0:NV, LANES * q : LANES * (q + 1)], operator[0:NV, :]], axis=1)
        keys = row_key[0:NV, :] ^ pair_irrep[q]
        folded = jnp.zeros((NV, LANES), F32)
        for t in range(0, TILES, 2):
            width = min(2, TILES - t)
            block = lax.dot_general(
                left, rhs[q, LANES * t : LANES * (t + width), :], NT, preferred_element_type=F32
            )
            for u in range(width):
                part = block[:, LANES * u : LANES * (u + 1)]
                folded = jnp.where(keys == col_key[t + u : t + u + 1, :], part, folded)
        scaled[q, 0:NV, :] = folded * inverse[q, 0:NV, :]

    def out_copy(i, slot):
        return pltpu.make_async_remote_copy(
            src_ref=out_send.at[i], dst_ref=out_recv.at[slot], send_sem=t_ssem.at[i],
            recv_sem=t_rsem.at[slot], device_id=on_plane(i, core), device_id_type=MESH,
        )

    scaled[:, NV:PADDED, :] = jnp.zeros((OWN, PADDED - NV, LANES), F32)

    def out_rows(j):
        for q in range(OWN):
            out_stage[OUT_HALF * q : OUT_HALF * (q + 1), :] = scaled[q, pl.ds(ROWS * j, OUT_HALF), :]
        return out_stage[...].astype(BF16)

    def out_step(k, carry):
        j = far_peer(k)

        @pl.when(j != ing)
        def _():
            out_send[j] = out_rows(j)
            out_copy(j, ing).start()

        return carry

    lax.fori_loop(0, RING, out_step, 0)
    out_recv[ing] = out_rows(ing)
    irreps_out[...] = g_recv[...]

    def sent(k, carry):
        i = plane_peer(k)
        g_copy(i, ing).wait_send()
        pack_copy(i, ing).wait_send()
        return carry

    lax.fori_loop(1, RING, sent, 0)

    def sent_pairs(k, carry):
        i, c = plane_peer(k // 2), (core + k) % 2
        red_copy(i, c, me).wait_send()
        op_copy(i, c, me).wait_send()
        return carry

    lax.fori_loop(1, PEERS, sent_pairs, 0)

    def sent_z(k, carry):
        z_copy((z + k) % DEPTH, z).wait_send()
        return carry

    lax.fori_loop(1, DEPTH, sent_z, 0)

    def out_wait(k, carry):
        j = plane_peer(k)
        out_copy(ing, j).wait_recv()
        out_copy(j, ing).wait_send()
        return carry

    lax.fori_loop(1, RING, out_wait, 0)
    result[...] = out_recv[...]


def expand_kernel(folded, irreps, row_key, irrep, update):
    keys = row_key[0:ROWS, :]
    for b in range(folded.shape[0]):
        values = folded[b].astype(F32)
        for q in range(OWN):
            part = values[OUT_HALF * q : OUT_HALF * q + ROWS, :]
            wanted = keys ^ irreps[b, q : q + 1, :]
            for t in range(TILES):
                width = min(LANES, NV - LANES * t)
                cols = slice(LANES * t, LANES * t + width)
                update[OWN * b + q, :, cols] = jnp.where(
                    wanted[:, 0:width] == irrep[:, cols], part[:, 0:width], 0.0
                )


def body(amplitudes, integrals, fock_block, virtual_irrep, pair_irrep, pair_energy, virtual_energy):
    vmem = pl.BlockSpec(memory_space=pltpu.VMEM)
    smem = pl.BlockSpec(memory_space=pltpu.SMEM)
    hbm = pl.BlockSpec(memory_space=pl.ANY)
    irrep = virtual_irrep.reshape(1, NV)
    dma = pltpu.SemaphoreType.DMA
    result, irreps, row_key = pl.pallas_call(
        main_kernel,
        name="residual",
        out_shape=(
            jax.ShapeDtypeStruct((RING, OUT_SLOT, LANES), BF16),
            jax.ShapeDtypeStruct((RING, OWN, LANES), I32),
            jax.ShapeDtypeStruct((OUT_HALF, LANES), I32),
        ),
        in_specs=[hbm, hbm, vmem, vmem, vmem, smem, smem],
        out_specs=(vmem, vmem, vmem),
        scratch_shapes=[
            pltpu.VMEM((GROUP_PAIRS, ROWS, NV), BF16),
            pltpu.VMEM((GROUP_PAIRS, ROWS, NV), BF16),
            pltpu.VMEM((8, LANES), I32),
            pltpu.VMEM((8, LANES), F32),
            pltpu.VMEM((PADDED, LANES), I32),
            pltpu.VMEM((PADDED, LANES), F32),
            pltpu.VMEM((OUT_HALF, LANES), I32),
            pltpu.VMEM((OWN, LANES), I32),
            pltpu.VMEM((RING, OWN, LANES), I32),
            pltpu.VMEM((IN_SLOT, LANES), F32),
            pltpu.VMEM((RING, IN_SLOT, LANES), BF16),
            pltpu.VMEM((RING, IN_SLOT, LANES), BF16),
            pltpu.VMEM((OWN, PADDED, LANES), F32),
            pltpu.VMEM((OWN, PADDED, LANES), F32),
            pltpu.VMEM((PADDED, 2 * LANES), BF16),
            pltpu.VMEM((OWN, PADDED, 2 * LANES), BF16),
            pltpu.VMEM((PADDED, 2 * LANES), BF16),
            pltpu.VMEM((2 * SLOT, LANES), F32),
            pltpu.VMEM((PADDED, LANES), F32),
            pltpu.VMEM((PEERS, SLOT, LANES), F32),
            pltpu.VMEM((PEERS, SLOT, LANES), F32),
            pltpu.VMEM((SLOT, LANES), F32),
            pltpu.VMEM((DEPTH, SLOT, LANES), F32),
            pltpu.VMEM((SLOT, LANES), BF16),
            pltpu.VMEM((PEERS, SLOT, LANES), BF16),
            pltpu.VMEM((PADDED, LANES), F32),
            pltpu.VMEM((OWN, PADDED, LANES), F32),
            pltpu.VMEM((OWN, PADDED, LANES), F32),
            pltpu.VMEM((OUT_SLOT, LANES), F32),
            pltpu.VMEM((RING, OUT_SLOT, LANES), BF16),
            pltpu.VMEM((RING, OUT_SLOT, LANES), BF16),
            dma((RING,)), dma((RING,)), dma((RING,)), dma((RING,)), dma((RING,)), dma((RING,)),
            dma((PEERS,)), dma((PEERS,)), dma((DEPTH,)), dma((DEPTH,)), dma((PEERS,)), dma((PEERS,)),
            dma((RING,)), dma((RING,)),
        ],
        compiler_params=pltpu.CompilerParams(collective_id=0, has_side_effects=True),
    )(amplitudes, integrals, fock_block, irrep, virtual_energy.reshape(1, NV), pair_irrep, pair_energy)

    step = 2
    return pl.pallas_call(
        expand_kernel,
        name="expand",
        grid=(RING // step,),
        out_shape=jax.ShapeDtypeStruct((GROUP_PAIRS, ROWS, NV), F32),
        in_specs=[
            pl.BlockSpec((step, OUT_SLOT, LANES), lambda j: (j, 0, 0)),
            pl.BlockSpec((step, OWN, LANES), lambda j: (j, 0, 0)),
            pl.BlockSpec((OUT_HALF, LANES), lambda j: (0, 0)),
            pl.BlockSpec((1, NV), lambda j: (0, 0)),
        ],
        out_specs=pl.BlockSpec((step * OWN, ROWS, NV), lambda j: (j, 0, 0)),
    )(result, irreps, row_key, irrep)


def solution(mesh):
    in_specs = (
        P("grp", "ing", None),
        P("grp", "ing", None),
        P("ing", None),
        P(),
        P(("grp", "ing")),
        P(("grp", "ing")),
        P(),
    )
    out_specs = P("grp", "ing", None)
    return jax.shard_map(body, mesh=mesh, in_specs=in_specs, out_specs=out_specs, check_vma=False)
```

```python
import functools

import jax
import jax.numpy as jnp
from jax import lax
from jax.experimental import pallas as pl
from jax.experimental.pallas import tpu as pltpu
from jax.sharding import PartitionSpec as P

NV, LANES, TILES = 800, 128, 7
PADDED = LANES * TILES
ROWS, OWN, GROUP_PAIRS = 50, 2, 32
GROUP = 8
RING, DEPTH, SIDE = 16, 8, 4
PEERS = 2 * RING
SLICE, SLOT = 25, 32
IN_SLOT, OUT_HALF, OUT_SLOT = 208, 56, 112
MESH = pl.DeviceIdType.MESH
F32, BF16, I32 = jnp.float32, jnp.bfloat16, jnp.int32
NT = (((1,), (1,)), ((), ()))


def tile_of(array, t):
    if t < TILES - 1:
        return array[:, LANES * t : LANES * (t + 1)]
    last = array[:, LANES * t : NV]
    pad = jnp.zeros((array.shape[0], PADDED - NV), array.dtype)
    return jnp.concatenate([last, pad], axis=1)


def main_kernel(
    amps, ints, fock, irrep, energy, pair_irrep, pair_energy,
    result, pair_key_out, own_wide_out, col_wide_out,
    amp_in, int_in, col_key, col_energy, row_key, row_energy, own_key, pair_key, fold_a, fold_b,
    g_send, g_recv, stage, pack_send, pack_recv, nat_a, nat_b, lhs, rhs, int_rhs,
    fock_fold, corr, red_send, red_recv, z_send, z_recv, op_send, op_recv, op_nat,
    inverse, scaled, out_stage, out_send, out_recv,
    amp_sem, int_sem, g_ssem, g_rsem, p_ssem, p_rsem, r_ssem, r_rsem,
    z_ssem, z_rsem, o_ssem, o_rsem, t_ssem, t_rsem,
):
    grp, ing = lax.axis_index("grp"), lax.axis_index("ing")
    z, core = grp // 2, grp % 2
    y, x = ing // SIDE, ing % SIDE
    me = ing * 2 + core

    def plane_peer(k):
        return ((y + k // SIDE) % SIDE) * SIDE + (x + k % SIDE) % SIDE

    def far_peer(k):
        return ((y + 2 + k // SIDE) % SIDE) * SIDE + (x + 2 + k % SIDE) % SIDE

    def on_plane(i, c):
        return (z * 2 + c, i)

    def chunk(h):
        place = pl.ds(GROUP * h, GROUP)
        return (
            pltpu.make_async_copy(amps.at[:, place], amp_in.at[h], amp_sem.at[h]),
            pltpu.make_async_copy(ints.at[:, place], int_in.at[h], int_sem.at[h]),
        )

    def load(k, carry):
        for copy in chunk((y + k) % SIDE):
            copy.start()
        return carry

    barrier = pltpu.get_barrier_semaphore()

    def greet(k, carry):
        pl.semaphore_signal(
            barrier, inc=1, device_id=on_plane(plane_peer(k // 2), (core + k) % 2), device_id_type=MESH
        )
        return carry

    def greet_z(k, carry):
        pl.semaphore_signal(
            barrier, inc=1, device_id=(((z + k) % DEPTH) * 2 + core, ing), device_id_type=MESH
        )
        return carry

    lax.fori_loop(1, PEERS, greet, 0)
    lax.fori_loop(1, DEPTH, greet_z, 0)
    lax.fori_loop(0, SIDE, load, 0)

    for q in range(OWN):
        g_send[q : q + 1, :] = jnp.full((1, LANES), pair_irrep[q], I32)
    g_recv[ing] = g_send[...]

    for t in range(TILES):
        if t < TILES - 1:
            col_key[t : t + 1, :] = irrep[LANES * t : LANES * (t + 1)].reshape(1, LANES)
            col_energy[t : t + 1, :] = energy[LANES * t : LANES * (t + 1)].reshape(1, LANES)
        else:
            col_key[t : t + 1, :] = jnp.full((1, LANES), -1, I32)
            col_key[t : t + 1, 0 : NV - LANES * t] = irrep[LANES * t : NV].reshape(1, NV - LANES * t)
            col_energy[t : t + 1, :] = jnp.zeros((1, LANES), F32)
            col_energy[t : t + 1, 0 : NV - LANES * t] = energy[LANES * t : NV].reshape(1, NV - LANES * t)
        col_wide_out[8 * t : 8 * (t + 1), :] = jnp.broadcast_to(col_key[t : t + 1, :], (8, LANES))
    for t in range(TILES):
        place = slice(LANES * t, LANES * (t + 1))
        keys = jnp.broadcast_to(col_key[t : t + 1, :].astype(F32), (LANES, LANES))
        row_key[place, :] = keys.T.astype(I32)
    own_key[...] = row_key[pl.ds(ROWS * ing, OUT_HALF), :]
    for a in range(ROWS):
        own_wide_out[8 * a : 8 * (a + 1), :] = jnp.broadcast_to(own_key[a : a + 1, :], (8, LANES))

    pl.semaphore_wait(barrier, PEERS - 1 + DEPTH - 1)

    def g_copy(i, slot, c=None):
        return pltpu.make_async_remote_copy(
            src_ref=g_send, dst_ref=g_recv.at[slot], send_sem=g_ssem.at[i], recv_sem=g_rsem.at[slot],
            device_id=on_plane(i, core), device_id_type=MESH,
        )

    def g_start(k, carry):
        g_copy(plane_peer(k), ing).start()
        return carry

    lax.fori_loop(1, RING, g_start, 0)

    def pack_copy(i, slot):
        return pltpu.make_async_remote_copy(
            src_ref=pack_send.at[i], dst_ref=pack_recv.at[slot], send_sem=p_ssem.at[i],
            recv_sem=p_rsem.at[slot], device_id=on_plane(i, core), device_id_type=MESH,
        )

    def fold_rows(h):
        pairs = pair_key[pl.ds(pl.multiple_of(GROUP * h, GROUP), GROUP), :]

        def some_rows(b, carry):
            for a in range(ROWS // 10):
                row = b * (ROWS // 10) + a
                place = pl.ds(pl.multiple_of(GROUP * row, GROUP), GROUP)
                wanted = own_wide_out[place, :] ^ pairs
                for source, folds in ((amp_in, fold_a), (int_in, fold_b)):
                    folded = jnp.zeros((GROUP, LANES), F32)
                    for t in range(TILES):
                        part = tile_of(source[h, row], t).astype(F32)
                        folded = jnp.where(wanted == col_wide_out[8 * t : 8 * (t + 1), :], part, folded)
                    folds[place, :] = folded
            return carry

        lax.fori_loop(0, 10, some_rows, 0)

    stage[4 * ROWS : IN_SLOT, :] = jnp.zeros((IN_SLOT - 4 * ROWS, LANES), F32)

    def pack_step(k, carry):
        h = (y + k) % SIDE
        for i in range(SIDE):
            j = SIDE * h + i

            @pl.when(j != ing)
            def _():
                g_copy(ing, j).wait_recv()

            pair_key[pl.ds(OWN * j, OWN), :] = g_recv[j]
        for copy in chunk(h):
            copy.wait()
        fold_rows(h)

        def pack_one(i, inner):
            place = (x + i) % SIDE
            j = SIDE * h + place
            for q in range(OWN):
                for which, folds in ((0, fold_a), (1, fold_b)):
                    first = ROWS * (which * OWN + q)
                    stage[first : first + ROWS, :] = folds[pl.ds(OWN * place + q, ROWS, stride=GROUP), :]
            packed = stage[...].astype(BF16)

            @pl.when(j != ing)
            def _():
                pack_send[j] = packed
                pack_copy(j, ing).start()

            @pl.when(j == ing)
            def _():
                pack_recv[j] = packed

            return inner

        lax.fori_loop(0, SIDE, pack_one, 0)
        return carry

    lax.fori_loop(0, SIDE, pack_step, 0)
    pair_key_out[...] = pair_key[...]

    fock_rows = fock[...].astype(F32)
    fock_keys = own_key[0:ROWS, :]
    folded_fock = jnp.zeros((ROWS, LANES), F32)
    for t in range(TILES):
        folded_fock = jnp.where(fock_keys == col_key[t : t + 1, :], tile_of(fock_rows, t), folded_fock)
    fock_fold[...] = jnp.zeros(fock_fold.shape, F32)
    fock_fold[0:ROWS, :] = folded_fock
    for t in range(TILES):
        place = slice(LANES * t, LANES * (t + 1))
        row_energy[place, :] = jnp.broadcast_to(col_energy[t : t + 1, :], (LANES, LANES)).T
    for q in range(OWN):
        for t in range(TILES):
            place = slice(LANES * t, LANES * (t + 1))
            wanted = row_key[place, :] ^ pair_irrep[q]
            other = jnp.zeros((LANES, LANES), F32)
            for u in range(TILES):
                other = jnp.where(wanted == col_key[u : u + 1, :], col_energy[u : u + 1, :], other)
            inverse[q, place, :] = 1.0 / (pair_energy[q] - row_energy[place, :] - other)
    nat_a[:, NV:PADDED, :] = jnp.zeros((OWN, PADDED - NV, LANES), F32)
    nat_b[:, NV:PADDED, :] = jnp.zeros((OWN, PADDED - NV, LANES), F32)
    op_nat[NV:PADDED, :] = jnp.zeros((PADDED - NV, LANES), F32)
    corr[NV:PADDED, :] = jnp.zeros((PADDED - NV, LANES), F32)

    def unpack(j):
        stage[...] = pack_recv[j].astype(F32)
        place = pl.ds(ROWS * j, ROWS)
        for q in range(OWN):
            nat_a[q, place, :] = stage[ROWS * q : ROWS * (q + 1), :]
            nat_b[q, place, :] = stage[ROWS * (OWN + q) : ROWS * (OWN + q + 1), :]

    unpack(ing)

    def unpack_step(k, carry):
        j = plane_peer(RING - k)
        pack_copy(ing, j).wait_recv()
        unpack(j)
        return carry

    lax.fori_loop(1, RING, unpack_step, 0)

    for q in range(OWN):
        lhs[:, LANES * q : LANES * (q + 1)] = nat_a[q].astype(BF16)
        int_rhs[:, LANES * q : LANES * (q + 1)] = nat_b[q].astype(BF16)
    for r in range(TILES):
        place = slice(LANES * r, LANES * (r + 1))
        low, high = max(r - 1, 0), min(r + 2, TILES)
        block = lax.dot_general(
            lhs[place, :], int_rhs[LANES * low : LANES * high, :], NT, preferred_element_type=F32
        )
        keys = row_key[place, :]
        folded = jnp.zeros((LANES, LANES), F32)
        for t in range(low, high):
            part = block[:, LANES * (t - low) : LANES * (t - low + 1)]
            folded = jnp.where(keys == col_key[t : t + 1, :], part, folded)
        corr[place, :] = folded

    def red_copy(i, c, slot):
        w = i * 2 + c
        return pltpu.make_async_remote_copy(
            src_ref=red_send.at[w], dst_ref=red_recv.at[slot], send_sem=r_ssem.at[w],
            recv_sem=r_rsem.at[slot], device_id=on_plane(i, c), device_id_type=MESH,
        )

    def red_step(k, carry):
        for c in range(2):
            i = far_peer(k)
            w = i * 2 + c
            rows = corr[pl.ds(SLICE * w, SLOT), :]

            @pl.when(w != me)
            def _():
                red_send[w] = rows
                red_copy(i, c, me).start()

            @pl.when(w == me)
            def _():
                red_recv[w] = rows

        return carry

    lax.fori_loop(0, RING, red_step, 0)

    for q in range(OWN):
        rhs[q, :, LANES : 2 * LANES] = (-nat_a[q]).astype(BF16)

    def red_wait(k, carry):
        i, c = plane_peer(k // 2), (core + k) % 2
        red_copy(ing, core, i * 2 + c).wait_recv()
        return carry

    lax.fori_loop(1, PEERS, red_wait, 0)
    total = red_recv[0]
    for w in range(1, PEERS):
        total = total + red_recv[w]
    z_send[...] = total

    def z_copy(dest, slot):
        return pltpu.make_async_remote_copy(
            src_ref=z_send, dst_ref=z_recv.at[slot], send_sem=z_ssem.at[dest],
            recv_sem=z_rsem.at[slot], device_id=(dest * 2 + core, ing), device_id_type=MESH,
        )

    def z_start(k, carry):
        z_copy((z + 3 + k) % DEPTH, z).start()
        return carry

    lax.fori_loop(1, 5, z_start, 0)
    lax.fori_loop(6, 9, z_start, 0)
    z_recv[z] = total

    def z_wait(k, carry):
        z_copy(z, (z + k) % DEPTH).wait_recv()
        return carry

    lax.fori_loop(1, DEPTH, z_wait, 0)
    total = z_recv[0]
    for k in range(1, DEPTH):
        total = total + z_recv[k]
    rows = (fock_fold[pl.ds(SLICE * core, SLOT), :] + total).astype(BF16)
    op_send[...] = rows
    op_recv[me] = rows

    def op_copy(i, c, slot):
        w = i * 2 + c
        return pltpu.make_async_remote_copy(
            src_ref=op_send, dst_ref=op_recv.at[slot], send_sem=o_ssem.at[w],
            recv_sem=o_rsem.at[slot], device_id=on_plane(i, c), device_id_type=MESH,
        )

    def op_start(k, carry):
        for c in range(2):
            i = far_peer(k)

            @pl.when(i * 2 + c != me)
            def _():
                op_copy(i, c, me).start()

        return carry

    lax.fori_loop(0, RING, op_start, 0)

    def op_place(w):
        op_nat[pl.ds(SLICE * w, SLICE), :] = op_recv[w].astype(F32)[0:SLICE, :]

    op_place(me)

    def op_wait(k, carry):
        w = plane_peer(k // 2) * 2 + (core + k) % 2
        op_copy(ing, core, w).wait_recv()
        op_place(w)
        return carry

    lax.fori_loop(1, PEERS, op_wait, 0)

    operator = op_nat[...].astype(BF16)
    for q in range(OWN):
        rhs[q, :, 0:LANES] = operator
        left = jnp.concatenate([lhs[0:NV, LANES * q : LANES * (q + 1)], operator[0:NV, :]], axis=1)
        keys = row_key[0:NV, :] ^ pair_irrep[q]
        folded = jnp.zeros((NV, LANES), F32)
        for t in range(0, TILES, 2):
            width = min(2, TILES - t)
            block = lax.dot_general(
                left, rhs[q, LANES * t : LANES * (t + width), :], NT, preferred_element_type=F32
            )
            for u in range(width):
                part = block[:, LANES * u : LANES * (u + 1)]
                folded = jnp.where(keys == col_key[t + u : t + u + 1, :], part, folded)
        scaled[q, 0:NV, :] = folded * inverse[q, 0:NV, :]

    def out_copy(i, slot):
        return pltpu.make_async_remote_copy(
            src_ref=out_send.at[i], dst_ref=out_recv.at[slot], send_sem=t_ssem.at[i],
            recv_sem=t_rsem.at[slot], device_id=on_plane(i, core), device_id_type=MESH,
        )

    scaled[:, NV:PADDED, :] = jnp.zeros((OWN, PADDED - NV, LANES), F32)

    def out_rows(j):
        for q in range(OWN):
            out_stage[OUT_HALF * q : OUT_HALF * (q + 1), :] = scaled[q, pl.ds(ROWS * j, OUT_HALF), :]
        return out_stage[...].astype(BF16)

    def out_step(k, carry):
        j = far_peer(k)

        @pl.when(j != ing)
        def _():
            out_send[j] = out_rows(j)
            out_copy(j, ing).start()

        return carry

    lax.fori_loop(0, RING, out_step, 0)
    out_recv[ing] = out_rows(ing)

    def sent(k, carry):
        i = plane_peer(k)
        g_copy(i, ing).wait_send()
        pack_copy(i, ing).wait_send()
        return carry

    lax.fori_loop(1, RING, sent, 0)

    def sent_pairs(k, carry):
        i, c = plane_peer(k // 2), (core + k) % 2
        red_copy(i, c, me).wait_send()
        op_copy(i, c, me).wait_send()
        return carry

    lax.fori_loop(1, PEERS, sent_pairs, 0)

    def sent_z(k, carry):
        z_copy((z + k) % DEPTH, z).wait_send()
        return carry

    lax.fori_loop(1, DEPTH, sent_z, 0)

    def spread(j):
        values = out_recv[j].astype(F32)
        for q in range(OWN):
            rows = values[OUT_HALF * q : OUT_HALF * q + ROWS, :]
            result[pl.ds(OWN * j + q, ROWS, stride=GROUP_PAIRS), :] = rows

    spread(ing)

    def out_wait(k, carry):
        j = plane_peer(RING - k)
        out_copy(ing, j).wait_recv()
        spread(j)
        out_copy(j, ing).wait_send()
        return carry

    lax.fori_loop(1, RING, out_wait, 0)


def expand_kernel(folded, pair_key, own_wide, col_wide, update):
    for a in range(update.shape[0]):
        for s in range(GROUP_PAIRS // GROUP):
            pairs = slice(GROUP * s, GROUP * (s + 1))
            wanted = pair_key[pairs, :] ^ own_wide[8 * a : 8 * (a + 1), :]
            values = folded[GROUP_PAIRS * a + GROUP * s : GROUP_PAIRS * a + GROUP * (s + 1), :]
            for t in range(TILES):
                width = min(LANES, NV - LANES * t)
                kept = jnp.where(wanted == col_wide[8 * t : 8 * (t + 1), :], values, 0.0)
                update[a, pairs, LANES * t : LANES * t + width] = kept[:, 0:width]


def body(amplitudes, integrals, fock_block, virtual_irrep, pair_irrep, pair_energy, virtual_energy):
    vmem = pl.BlockSpec(memory_space=pltpu.VMEM)
    smem = pl.BlockSpec(memory_space=pltpu.SMEM)
    hbm = pl.BlockSpec(memory_space=pl.ANY)
    dma = pltpu.SemaphoreType.DMA
    result, pair_key, own_wide, col_wide = pl.pallas_call(
        main_kernel,
        name="residual",
        out_shape=(
            jax.ShapeDtypeStruct((ROWS * GROUP_PAIRS, LANES), F32),
            jax.ShapeDtypeStruct((GROUP_PAIRS, LANES), I32),
            jax.ShapeDtypeStruct((ROWS * 8, LANES), I32),
            jax.ShapeDtypeStruct((TILES * 8, LANES), I32),
        ),
        in_specs=[hbm, hbm, vmem, vmem, vmem, smem, smem],
        out_specs=(vmem, vmem, vmem, vmem),
        scratch_shapes=[
            pltpu.VMEM((GROUP_PAIRS // GROUP, ROWS, GROUP, NV), BF16),
            pltpu.VMEM((GROUP_PAIRS // GROUP, ROWS, GROUP, NV), BF16),
            pltpu.VMEM((8, LANES), I32),
            pltpu.VMEM((8, LANES), F32),
            pltpu.VMEM((PADDED, LANES), I32),
            pltpu.VMEM((PADDED, LANES), F32),
            pltpu.VMEM((OUT_HALF, LANES), I32),
            pltpu.VMEM((GROUP_PAIRS, LANES), I32),
            pltpu.VMEM((ROWS * GROUP, LANES), F32),
            pltpu.VMEM((ROWS * GROUP, LANES), F32),
            pltpu.VMEM((OWN, LANES), I32),
            pltpu.VMEM((RING, OWN, LANES), I32),
            pltpu.VMEM((IN_SLOT, LANES), F32),
            pltpu.VMEM((RING, IN_SLOT, LANES), BF16),
            pltpu.VMEM((RING, IN_SLOT, LANES), BF16),
            pltpu.VMEM((OWN, PADDED, LANES), F32),
            pltpu.VMEM((OWN, PADDED, LANES), F32),
            pltpu.VMEM((PADDED, 2 * LANES), BF16),
            pltpu.VMEM((OWN, PADDED, 2 * LANES), BF16),
            pltpu.VMEM((PADDED, 2 * LANES), BF16),
            pltpu.VMEM((2 * SLOT, LANES), F32),
            pltpu.VMEM((PADDED, LANES), F32),
            pltpu.VMEM((PEERS, SLOT, LANES), F32),
            pltpu.VMEM((PEERS, SLOT, LANES), F32),
            pltpu.VMEM((SLOT, LANES), F32),
            pltpu.VMEM((DEPTH, SLOT, LANES), F32),
            pltpu.VMEM((SLOT, LANES), BF16),
            pltpu.VMEM((PEERS, SLOT, LANES), BF16),
            pltpu.VMEM((PADDED, LANES), F32),
            pltpu.VMEM((OWN, PADDED, LANES), F32),
            pltpu.VMEM((OWN, PADDED, LANES), F32),
            pltpu.VMEM((OUT_SLOT, LANES), F32),
            pltpu.VMEM((RING, OUT_SLOT, LANES), BF16),
            pltpu.VMEM((RING, OUT_SLOT, LANES), BF16),
            dma((SIDE,)), dma((SIDE,)), dma((RING,)), dma((RING,)), dma((RING,)), dma((RING,)),
            dma((PEERS,)), dma((PEERS,)), dma((DEPTH,)), dma((DEPTH,)), dma((PEERS,)), dma((PEERS,)),
            dma((RING,)), dma((RING,)),
        ],
        compiler_params=pltpu.CompilerParams(collective_id=0, has_side_effects=True),
    )(
        jnp.transpose(amplitudes, (1, 0, 2)), jnp.transpose(integrals, (1, 0, 2)), fock_block,
        virtual_irrep, virtual_energy, pair_irrep, pair_energy,
    )

    step = 25
    update = pl.pallas_call(
        expand_kernel,
        name="expand",
        grid=(ROWS // step,),
        out_shape=jax.ShapeDtypeStruct((ROWS, GROUP_PAIRS, NV), F32),
        in_specs=[
            pl.BlockSpec((step * GROUP_PAIRS, LANES), lambda j: (j, 0)),
            pl.BlockSpec((GROUP_PAIRS, LANES), lambda j: (0, 0)),
            pl.BlockSpec((step * 8, LANES), lambda j: (j, 0)),
            pl.BlockSpec((TILES * 8, LANES), lambda j: (0, 0)),
        ],
        out_specs=pl.BlockSpec((step, GROUP_PAIRS, NV), lambda j: (j, 0, 0)),
    )(result, pair_key, own_wide, col_wide)
    return jnp.transpose(update, (1, 0, 2))


def solution(mesh):
    in_specs = (
        P("grp", "ing", None),
        P("grp", "ing", None),
        P("ing", None),
        P(),
        P(("grp", "ing")),
        P(("grp", "ing")),
        P(),
    )
    out_specs = P("grp", "ing", None)
    return jax.shard_map(body, mesh=mesh, in_specs=in_specs, out_specs=out_specs, check_vma=False)
```

```python
import functools

import jax
import jax.numpy as jnp
from jax import lax
from jax.experimental import pallas as pl
from jax.experimental.pallas import tpu as pltpu
from jax.sharding import PartitionSpec as P

NV, LANES, TILES = 800, 128, 7
PADDED = LANES * TILES
ROWS, OWN, GROUP_PAIRS = 50, 2, 32
GROUP = 16
HALVES = GROUP_PAIRS // GROUP
RING, DEPTH, SIDE = 16, 8, 4
PEERS = 2 * RING
SLICE, SLOT = 26, 32
WIDE = 56
MESH = pl.DeviceIdType.MESH
F32, BF16, I32 = jnp.float32, jnp.bfloat16, jnp.int32
NT = (((1,), (1,)), ((), ()))


def tile_of(array, t):
    if t < TILES - 1:
        return array[:, LANES * t : LANES * (t + 1)]
    last = array[:, LANES * t : NV]
    pad = jnp.zeros((array.shape[0], PADDED - NV), array.dtype)
    return jnp.concatenate([last, pad], axis=1)


def main_kernel(
    amps, ints, fock, irrep, energy, pair_irrep, pair_energy,
    result, pair_key_out, own_wide_out, col_wide_out,
    amp_in, int_in, col_key, col_half, col_energy, row_key, row_energy, own_key, pair_key,
    g_send, g_recv, fold, pack_recv, mixed, lhs, rhs, int_rhs,
    fock_fold, corr, red_recv, z_send, z_recv, op_send, op_all,
    inverse, out_send, out_recv,
    amp_sem, int_sem, g_ssem, g_rsem, p_ssem, p_rsem, r_ssem, r_rsem,
    z_ssem, z_rsem, o_ssem, o_rsem, t_ssem, t_rsem, own_sem,
):
    grp, ing = lax.axis_index("grp"), lax.axis_index("ing")
    z, core = grp // 2, grp % 2
    y, x = ing // SIDE, ing % SIDE
    me = ing * 2 + core

    def plane_peer(k):
        return ((y + k // SIDE) % SIDE) * SIDE + (x + k % SIDE) % SIDE

    def far_peer(k):
        return ((y + 2 + k // SIDE) % SIDE) * SIDE + (x + 2 + k % SIDE) % SIDE

    def on_plane(i, c):
        return (z * 2 + c, i)

    def chunk(h):
        place = pl.ds(GROUP * h, GROUP)
        return (
            pltpu.make_async_copy(amps.at[:, place], amp_in.at[h], amp_sem.at[h]),
            pltpu.make_async_copy(ints.at[:, place], int_in.at[h], int_sem.at[h]),
        )

    def load(k, carry):
        for copy in chunk((y // 2 + k) % HALVES):
            copy.start()
        return carry

    barrier = pltpu.get_barrier_semaphore()

    def greet(k, carry):
        pl.semaphore_signal(
            barrier, inc=1, device_id=on_plane(plane_peer(k // 2), (core + k) % 2), device_id_type=MESH
        )
        return carry

    def greet_z(k, carry):
        pl.semaphore_signal(
            barrier, inc=1, device_id=(((z + k) % DEPTH) * 2 + core, ing), device_id_type=MESH
        )
        return carry

    lax.fori_loop(1, PEERS, greet, 0)
    lax.fori_loop(1, DEPTH, greet_z, 0)
    lax.fori_loop(0, HALVES, load, 0)

    for q in range(OWN):
        g_send[q : q + 1, :] = jnp.full((1, LANES), pair_irrep[q], I32)
    g_recv[ing] = g_send[...]

    pl.semaphore_wait(barrier, PEERS - 1 + DEPTH - 1)

    def g_copy(i, slot, c=None):
        return pltpu.make_async_remote_copy(
            src_ref=g_send, dst_ref=g_recv.at[slot], send_sem=g_ssem.at[i], recv_sem=g_rsem.at[slot],
            device_id=on_plane(i, core), device_id_type=MESH,
        )

    def g_start(k, carry):
        g_copy(plane_peer(k), ing).start()
        return carry

    lax.fori_loop(1, RING, g_start, 0)

    for t in range(TILES):
        if t < TILES - 1:
            col_key[t : t + 1, :] = irrep[LANES * t : LANES * (t + 1)].reshape(1, LANES)
            col_energy[t : t + 1, :] = energy[LANES * t : LANES * (t + 1)].reshape(1, LANES)
        else:
            col_key[t : t + 1, :] = jnp.full((1, LANES), -1, I32)
            col_key[t : t + 1, 0 : NV - LANES * t] = irrep[LANES * t : NV].reshape(1, NV - LANES * t)
            col_energy[t : t + 1, :] = jnp.zeros((1, LANES), F32)
            col_energy[t : t + 1, 0 : NV - LANES * t] = energy[LANES * t : NV].reshape(1, NV - LANES * t)
        col_wide_out[8 * t : 8 * (t + 1), :] = jnp.broadcast_to(col_key[t : t + 1, :], (8, LANES))
        col_half[GROUP * t : GROUP * (t + 1), :] = jnp.broadcast_to(
            col_key[t : t + 1, :].astype(F32), (GROUP, LANES)
        ).astype(BF16)
    for t in range(TILES):
        place = slice(LANES * t, LANES * (t + 1))
        keys = jnp.broadcast_to(col_key[t : t + 1, :].astype(F32), (LANES, LANES))
        row_key[place, :] = keys.T.astype(I32)
    own_key[...] = row_key[pl.ds(ROWS * ing, WIDE), :]
    for a in range(ROWS):
        own_wide_out[8 * a : 8 * (a + 1), :] = jnp.broadcast_to(own_key[a : a + 1, :], (8, LANES))

    def pack_copy(i, slot):
        return pltpu.make_async_remote_copy(
            src_ref=fold.at[:, :, pl.ds(OWN * i, OWN), :], dst_ref=pack_recv.at[:, pl.ds(ROWS * slot, ROWS)],
            send_sem=p_ssem.at[i], recv_sem=p_rsem.at[slot], device_id=on_plane(i, core),
            device_id_type=MESH,
        )

    def fold_rows(h):
        pairs = pair_key[pl.ds(pl.multiple_of(GROUP * h, GROUP), GROUP), :]
        place = pl.ds(pl.multiple_of(GROUP * h, GROUP), GROUP)

        def some_rows(b, carry):
            for a in range(ROWS // 10):
                row = b * (ROWS // 10) + a
                key = own_wide_out[pl.ds(pl.multiple_of(8 * row, 8), 8), :]
                wanted = (jnp.concatenate([key, key], axis=0) ^ pairs).astype(F32).astype(BF16)
                for which, source in ((0, amp_in), (1, int_in)):
                    folded = jnp.zeros((GROUP, LANES), BF16)
                    for t in range(TILES):
                        part = tile_of(source[h, row], t)
                        folded = jnp.where(wanted == col_half[GROUP * t : GROUP * (t + 1), :], part, folded)
                    fold[which, row, place, :] = folded
            return carry

        lax.fori_loop(0, 10, some_rows, 0)

    own_rows = pltpu.make_async_copy(
        fold.at[:, :, pl.ds(OWN * ing, OWN), :], pack_recv.at[:, pl.ds(ROWS * ing, ROWS)], own_sem.at[0]
    )

    def pack_step(k, carry):
        h = (y // 2 + k) % HALVES
        for i in range(RING // HALVES):
            j = RING // HALVES * h + i

            @pl.when(j != ing)
            def _():
                g_copy(ing, j).wait_recv()

            pair_key[pl.ds(OWN * j, OWN), :] = g_recv[j]
        for copy in chunk(h):
            copy.wait()
        fold_rows(h)
        for i in range(RING // HALVES):
            j = RING // HALVES * h + i

            @pl.when(j != ing)
            def _():
                pack_copy(j, ing).start()

            @pl.when(j == ing)
            def _():
                own_rows.start()

        return carry

    lax.fori_loop(0, HALVES, pack_step, 0)
    pair_key_out[...] = pair_key[...]

    fock_rows = fock[...].astype(F32)
    fock_keys = own_key[0:ROWS, :]
    folded_fock = jnp.zeros((ROWS, LANES), F32)
    for t in range(TILES):
        folded_fock = jnp.where(fock_keys == col_key[t : t + 1, :], tile_of(fock_rows, t), folded_fock)
    fock_fold[...] = jnp.zeros(fock_fold.shape, F32)
    fock_fold[0:ROWS, :] = folded_fock
    for t in range(TILES):
        place = slice(LANES * t, LANES * (t + 1))
        row_energy[place, :] = jnp.broadcast_to(col_energy[t : t + 1, :], (LANES, LANES)).T
    for q in range(OWN):
        for t in range(TILES):
            place = slice(LANES * t, LANES * (t + 1))
            wanted = row_key[place, :] ^ pair_irrep[q]
            other = jnp.zeros((LANES, LANES), F32)
            for u in range(TILES):
                other = jnp.where(wanted == col_key[u : u + 1, :], col_energy[u : u + 1, :], other)
            inverse[q, place, :] = 1.0 / (pair_energy[q] - row_energy[place, :] - other)
    lhs[NV:PADDED, :] = jnp.zeros((PADDED - NV, 2 * LANES), BF16)
    int_rhs[NV:PADDED, :] = jnp.zeros((PADDED - NV, 2 * LANES), BF16)
    rhs[:, NV:PADDED, :] = jnp.zeros((OWN, PADDED - NV, 2 * LANES), BF16)

    own_rows.wait()

    def pack_wait(k, carry):
        pack_copy(ing, plane_peer(RING - k)).wait_recv()
        return carry

    lax.fori_loop(1, RING, pack_wait, 0)
    for which, target in ((0, lhs), (1, int_rhs)):
        mixed[...] = pack_recv[which].reshape(OWN * NV, LANES).astype(F32)
        for q in range(OWN):
            target[0:NV, LANES * q : LANES * (q + 1)] = mixed[pl.ds(q, NV, stride=OWN), :].astype(BF16)

    for r in range(TILES):
        place = slice(LANES * r, LANES * (r + 1))
        low, high = max(r - 1, 0), min(r + 2, TILES)
        block = lax.dot_general(
            lhs[place, :], int_rhs[LANES * low : LANES * high, :], NT, preferred_element_type=F32
        )
        keys = row_key[place, :]
        folded = jnp.zeros((LANES, LANES), F32)
        for t in range(low, high):
            part = block[:, LANES * (t - low) : LANES * (t - low + 1)]
            folded = jnp.where(keys == col_key[t : t + 1, :], part, folded)
        corr[place, :] = folded

    def red_copy(i, c, slot):
        return pltpu.make_async_remote_copy(
            src_ref=corr.at[pl.ds(ROWS * i + SLICE * c, SLICE)], dst_ref=red_recv.at[slot, pl.ds(0, SLICE)],
            send_sem=r_ssem.at[i * 2 + c], recv_sem=r_rsem.at[slot], device_id=on_plane(i, c),
            device_id_type=MESH,
        )

    def red_step(k, carry):
        for c in range(2):
            i = far_peer(k)

            @pl.when(i * 2 + c != me)
            def _():
                red_copy(i, c, me).start()

        return carry

    lax.fori_loop(0, RING, red_step, 0)
    red_recv[me, 0:SLICE, :] = corr[pl.ds(ROWS * ing + SLICE * core, SLICE), :]

    for q in range(OWN):
        rhs[q, 0:NV, LANES : 2 * LANES] = -lhs[0:NV, LANES * q : LANES * (q + 1)]

    def red_wait(k, carry):
        i, c = plane_peer(k // 2), (core + k) % 2
        red_copy(ing, core, i * 2 + c).wait_recv()
        return carry

    lax.fori_loop(1, PEERS, red_wait, 0)
    total = red_recv[0, 0:SLICE, :]
    for w in range(1, PEERS):
        total = total + red_recv[w, 0:SLICE, :]
    z_send[0:SLICE, :] = total

    def z_copy(dest, slot):
        return pltpu.make_async_remote_copy(
            src_ref=z_send.at[pl.ds(0, SLICE)], dst_ref=z_recv.at[slot, pl.ds(0, SLICE)], send_sem=z_ssem.at[dest],
            recv_sem=z_rsem.at[slot], device_id=(dest * 2 + core, ing), device_id_type=MESH,
        )

    def z_start(k, carry):
        z_copy((z + 3 + k) % DEPTH, z).start()
        return carry

    lax.fori_loop(1, 5, z_start, 0)
    lax.fori_loop(6, 9, z_start, 0)
    z_recv[z, 0:SLICE, :] = total

    def z_wait(k, carry):
        z_copy(z, (z + k) % DEPTH).wait_recv()
        return carry

    lax.fori_loop(1, DEPTH, z_wait, 0)
    total = z_recv[0, 0:SLICE, :]
    for k in range(1, DEPTH):
        total = total + z_recv[k, 0:SLICE, :]
    op_send[0:SLICE, :] = (fock_fold[pl.ds(SLICE * core, SLICE), :] + total).astype(BF16)

    def op_rows(c):
        return SLICE if c == 0 else ROWS - SLICE

    def op_copy(i, c, source, source_core):
        rows = op_rows(source_core)
        return pltpu.make_async_remote_copy(
            src_ref=op_send.at[pl.ds(0, rows)], dst_ref=op_all.at[pl.ds(ROWS * source + SLICE * source_core, rows)],
            send_sem=o_ssem.at[i * 2 + c], recv_sem=o_rsem.at[source * 2 + source_core],
            device_id=on_plane(i, c), device_id_type=MESH,
        )

    for mine in range(2):

        @pl.when(core == mine)
        def _():
            def op_start(k, carry):
                for c in range(2):
                    i = far_peer(k)

                    @pl.when(i * 2 + c != me)
                    def _():
                        op_copy(i, c, ing, mine).start()

                return carry

            lax.fori_loop(0, RING, op_start, 0)
            own_op = pltpu.make_async_copy(
                op_send.at[pl.ds(0, op_rows(mine))],
                op_all.at[pl.ds(ROWS * ing + SLICE * mine, op_rows(mine))], own_sem.at[1],
            )
            own_op.start()
            own_op.wait()

    def op_wait(k, carry):
        for c in range(2):
            i = plane_peer(k)

            @pl.when(i * 2 + c != me)
            def _():
                op_copy(ing, core, i, c).wait_recv()

        return carry

    lax.fori_loop(0, RING, op_wait, 0)

    operator = op_all[...]
    for q in range(OWN):
        rhs[q, 0:NV, 0:LANES] = operator
        left = jnp.concatenate([lhs[0:NV, LANES * q : LANES * (q + 1)], operator], axis=1)
        keys = row_key[0:NV, :] ^ pair_irrep[q]
        folded = jnp.zeros((NV, LANES), F32)
        for t in range(0, TILES, 2):
            width = min(2, TILES - t)
            block = lax.dot_general(
                left, rhs[q, LANES * t : LANES * (t + width), :], NT, preferred_element_type=F32
            )
            for u in range(width):
                part = block[:, LANES * u : LANES * (u + 1)]
                folded = jnp.where(keys == col_key[t + u : t + u + 1, :], part, folded)
        mixed[pl.ds(q, NV, stride=OWN), :] = folded * inverse[q, 0:NV, :]
    out_send[...] = mixed[...].astype(BF16).reshape(NV, OWN, LANES)

    def out_copy(i, slot):
        return pltpu.make_async_remote_copy(
            src_ref=out_send.at[pl.ds(ROWS * i, ROWS)], dst_ref=out_recv.at[:, pl.ds(OWN * slot, OWN), :],
            send_sem=t_ssem.at[i], recv_sem=t_rsem.at[slot], device_id=on_plane(i, core),
            device_id_type=MESH,
        )

    def out_step(k, carry):
        j = far_peer(k)

        @pl.when(j != ing)
        def _():
            out_copy(j, ing).start()

        return carry

    lax.fori_loop(0, RING, out_step, 0)
    own_out = pltpu.make_async_copy(
        out_send.at[pl.ds(ROWS * ing, ROWS)], out_recv.at[:, pl.ds(OWN * ing, OWN), :], own_sem.at[2]
    )
    own_out.start()

    def sent(k, carry):
        i = plane_peer(k)
        g_copy(i, ing).wait_send()
        pack_copy(i, ing).wait_send()
        return carry

    lax.fori_loop(1, RING, sent, 0)

    def sent_pairs(k, carry):
        i, c = plane_peer(k // 2), (core + k) % 2
        red_copy(i, c, me).wait_send()
        return carry

    lax.fori_loop(1, PEERS, sent_pairs, 0)

    for mine in range(2):

        @pl.when(core == mine)
        def _():
            def sent_op(k, carry):
                i, c = plane_peer(k // 2), (core + k) % 2
                op_copy(i, c, ing, mine).wait_send()
                return carry

            lax.fori_loop(1, PEERS, sent_op, 0)

    def sent_z(k, carry):
        z_copy((z + k) % DEPTH, z).wait_send()
        return carry

    lax.fori_loop(1, DEPTH, sent_z, 0)

    own_out.wait()

    def out_wait(k, carry):
        j = plane_peer(RING - k)
        out_copy(ing, j).wait_recv()
        out_copy(j, ing).wait_send()
        return carry

    lax.fori_loop(1, RING, out_wait, 0)
    result[...] = out_recv[...]


def expand_kernel(folded, pair_key, own_wide, col_wide, update):
    for a in range(update.shape[0]):
        for s in range(GROUP_PAIRS // 8):
            pairs = slice(8 * s, 8 * (s + 1))
            wanted = pair_key[pairs, :] ^ own_wide[8 * a : 8 * (a + 1), :]
            values = folded[a, pairs, :].astype(F32)
            for t in range(TILES):
                width = min(LANES, NV - LANES * t)
                kept = jnp.where(wanted == col_wide[8 * t : 8 * (t + 1), :], values, 0.0)
                update[a, pairs, LANES * t : LANES * t + width] = kept[:, 0:width]


def body(amplitudes, integrals, fock_block, virtual_irrep, pair_irrep, pair_energy, virtual_energy):
    vmem = pl.BlockSpec(memory_space=pltpu.VMEM)
    smem = pl.BlockSpec(memory_space=pltpu.SMEM)
    hbm = pl.BlockSpec(memory_space=pl.ANY)
    dma = pltpu.SemaphoreType.DMA
    result, pair_key, own_wide, col_wide = pl.pallas_call(
        main_kernel,
        name="residual",
        out_shape=(
            jax.ShapeDtypeStruct((ROWS, GROUP_PAIRS, LANES), BF16),
            jax.ShapeDtypeStruct((GROUP_PAIRS, LANES), I32),
            jax.ShapeDtypeStruct((ROWS * 8, LANES), I32),
            jax.ShapeDtypeStruct((TILES * 8, LANES), I32),
        ),
        in_specs=[hbm, hbm, vmem, vmem, vmem, smem, smem],
        out_specs=(vmem, vmem, vmem, vmem),
        scratch_shapes=[
            pltpu.VMEM((HALVES, ROWS, GROUP, NV), BF16),
            pltpu.VMEM((HALVES, ROWS, GROUP, NV), BF16),
            pltpu.VMEM((8, LANES), I32),
            pltpu.VMEM((TILES * GROUP, LANES), BF16),
            pltpu.VMEM((8, LANES), F32),
            pltpu.VMEM((PADDED, LANES), I32),
            pltpu.VMEM((PADDED, LANES), F32),
            pltpu.VMEM((WIDE, LANES), I32),
            pltpu.VMEM((GROUP_PAIRS, LANES), I32),
            pltpu.VMEM((OWN, LANES), I32),
            pltpu.VMEM((RING, OWN, LANES), I32),
            pltpu.VMEM((2, ROWS, GROUP_PAIRS, LANES), BF16),
            pltpu.VMEM((2, NV, OWN, LANES), BF16),
            pltpu.VMEM((OWN * NV, LANES), F32),
            pltpu.VMEM((PADDED, 2 * LANES), BF16),
            pltpu.VMEM((OWN, PADDED, 2 * LANES), BF16),
            pltpu.VMEM((PADDED, 2 * LANES), BF16),
            pltpu.VMEM((2 * SLOT, LANES), F32),
            pltpu.VMEM((PADDED, LANES), F32),
            pltpu.VMEM((PEERS, SLOT, LANES), F32),
            pltpu.VMEM((SLOT, LANES), F32),
            pltpu.VMEM((DEPTH, SLOT, LANES), F32),
            pltpu.VMEM((SLOT, LANES), BF16),
            pltpu.VMEM((NV, LANES), BF16),
            pltpu.VMEM((OWN, PADDED, LANES), F32),
            pltpu.VMEM((NV, OWN, LANES), BF16),
            pltpu.VMEM((ROWS, GROUP_PAIRS, LANES), BF16),
            dma((HALVES,)), dma((HALVES,)), dma((RING,)), dma((RING,)), dma((RING,)), dma((RING,)),
            dma((PEERS,)), dma((PEERS,)), dma((DEPTH,)), dma((DEPTH,)), dma((PEERS,)), dma((PEERS,)),
            dma((RING,)), dma((RING,)), dma((3,)),
        ],
        compiler_params=pltpu.CompilerParams(collective_id=0, has_side_effects=True),
    )(
        jnp.transpose(amplitudes, (1, 0, 2)), jnp.transpose(integrals, (1, 0, 2)), fock_block,
        virtual_irrep, virtual_energy, pair_irrep, pair_energy,
    )

    step = 25
    update = pl.pallas_call(
        expand_kernel,
        name="expand",
        grid=(ROWS // step,),
        out_shape=jax.ShapeDtypeStruct((ROWS, GROUP_PAIRS, NV), F32),
        in_specs=[
            pl.BlockSpec((step, GROUP_PAIRS, LANES), lambda j: (j, 0, 0)),
            pl.BlockSpec((GROUP_PAIRS, LANES), lambda j: (0, 0)),
            pl.BlockSpec((step * 8, LANES), lambda j: (j, 0)),
            pl.BlockSpec((TILES * 8, LANES), lambda j: (0, 0)),
        ],
        out_specs=pl.BlockSpec((step, GROUP_PAIRS, NV), lambda j: (j, 0, 0)),
    )(result, pair_key, own_wide, col_wide)
    return jnp.transpose(update, (1, 0, 2))


def solution(mesh):
    in_specs = (
        P("grp", "ing", None),
        P("grp", "ing", None),
        P("ing", None),
        P(),
        P(("grp", "ing")),
        P(("grp", "ing")),
        P(),
    )
    out_specs = P("grp", "ing", None)
    return jax.shard_map(body, mesh=mesh, in_specs=in_specs, out_specs=out_specs, check_vma=False)
```

```python
import functools

import jax
import jax.numpy as jnp
from jax import lax
from jax.experimental import pallas as pl
from jax.experimental.pallas import tpu as pltpu
from jax.sharding import PartitionSpec as P

NV, LANES, TILES = 800, 128, 7
PADDED = LANES * TILES
ROWS, OWN, GROUP_PAIRS = 50, 2, 32
GROUP = 16
HALVES = GROUP_PAIRS // GROUP
RING, DEPTH, SIDE = 16, 8, 4
PEERS = 2 * RING
SLICE, SLOT = 26, 32
WIDE = 56
MESH = pl.DeviceIdType.MESH
F32, BF16, I32 = jnp.float32, jnp.bfloat16, jnp.int32
NT = (((1,), (1,)), ((), ()))


def tile_of(array, t):
    if t < TILES - 1:
        return array[:, LANES * t : LANES * (t + 1)]
    last = array[:, LANES * t : NV]
    pad = jnp.zeros((array.shape[0], PADDED - NV), array.dtype)
    return jnp.concatenate([last, pad], axis=1)


def main_kernel(
    amps, ints, fock_in, irrep_in, energy_in, pair_irrep_in, pair_energy_in,
    result, pair_key_out, own_wide_out, col_wide_out,
    fock, irrep, energy, pair_irrep, pair_energy, own_wide, col_wide,
    amp_in, int_in, col_key, col_half, col_energy, row_key, row_energy, own_key, pair_key,
    g_send, g_recv, fold, pack_recv, mixed, lhs, rhs, int_rhs,
    fock_fold, corr, red_recv, z_send, z_recv, op_send, op_all,
    inverse, out_send, out_recv,
    amp_sem, int_sem, g_ssem, g_rsem, p_ssem, p_rsem, r_ssem, r_rsem,
    z_ssem, z_rsem, o_ssem, o_rsem, t_ssem, t_rsem, own_sem, in_sem, key_sem,
):
    grp, ing = lax.axis_index("grp"), lax.axis_index("ing")
    z, core = grp // 2, grp % 2
    y, x = ing // SIDE, ing % SIDE
    me = ing * 2 + core

    beside = y + 1 - 2 * (y % 2)
    across = [y, beside, (y + 2) % SIDE, (beside + 2) % SIDE]
    along = [(x + k) % SIDE for k in range(SIDE)]
    peer = {(r, k): across[r] * SIDE + along[k] for r in range(SIDE) for k in range(SIDE)}
    hops = {(r, k): (0, 1, 2, 1)[r] + (0, 1, 2, 1)[k] for r in range(SIDE) for k in range(SIDE)}
    near = [at for at in sorted(peer, key=hops.get) if at != (0, 0)]
    far = near[::-1]
    sibling = 1 - core
    above = {k: (z + k) % DEPTH for k in (4, 3, 5, 2, 6, 1, 7)}

    def on_plane(i, c):
        return (z * 2 + c, i)

    def chunk(h):
        place = pl.ds(GROUP * h, GROUP)
        return (
            pltpu.make_async_copy(amps.at[:, place], amp_in.at[h], amp_sem.at[h]),
            pltpu.make_async_copy(ints.at[:, place], int_in.at[h], int_sem.at[h]),
        )

    small = [
        pltpu.make_async_copy(source, target, in_sem.at[n])
        for n, (source, target) in enumerate(
            ((pair_irrep_in, pair_irrep), (irrep_in, irrep), (energy_in, energy),
             (pair_energy_in, pair_energy), (fock_in, fock))
        )
    ]
    for copy in small:
        copy.start()

    barrier = pltpu.get_barrier_semaphore()

    def greet(g, i):
        pl.semaphore_signal(barrier, inc=1, device_id=(g, i), device_id_type=MESH)

    for at in far:
        greet(z * 2 + core, peer[at])
        greet(z * 2 + sibling, peer[at])
    greet(z * 2 + sibling, ing)
    for k in above:
        greet(above[k] * 2 + core, ing)

    halves = [y // 2, 1 - y // 2]
    for h in halves:
        for copy in chunk(h):
            copy.start()
    small[0].wait()

    for q in range(OWN):
        g_send[q : q + 1, :] = jnp.full((1, LANES), pair_irrep[q], I32)
    g_recv[ing] = g_send[...]

    pl.semaphore_wait(barrier, PEERS - 1 + DEPTH - 1)

    def g_copy(i, slot, c=None):
        return pltpu.make_async_remote_copy(
            src_ref=g_send, dst_ref=g_recv.at[slot], send_sem=g_ssem.at[i], recv_sem=g_rsem.at[slot],
            device_id=on_plane(i, core), device_id_type=MESH,
        )

    for at in far:
        g_copy(peer[at], ing).start()
    for copy in small[1:]:
        copy.wait()

    for t in range(TILES):
        if t < TILES - 1:
            col_key[t : t + 1, :] = irrep[LANES * t : LANES * (t + 1)].reshape(1, LANES)
            col_energy[t : t + 1, :] = energy[LANES * t : LANES * (t + 1)].reshape(1, LANES)
        else:
            col_key[t : t + 1, :] = jnp.full((1, LANES), -1, I32)
            col_key[t : t + 1, 0 : NV - LANES * t] = irrep[LANES * t : NV].reshape(1, NV - LANES * t)
            col_energy[t : t + 1, :] = jnp.zeros((1, LANES), F32)
            col_energy[t : t + 1, 0 : NV - LANES * t] = energy[LANES * t : NV].reshape(1, NV - LANES * t)
        col_wide[8 * t : 8 * (t + 1), :] = jnp.broadcast_to(col_key[t : t + 1, :], (8, LANES))
        col_half[GROUP * t : GROUP * (t + 1), :] = jnp.broadcast_to(
            col_key[t : t + 1, :].astype(F32), (GROUP, LANES)
        ).astype(BF16)
    for t in range(TILES):
        place = slice(LANES * t, LANES * (t + 1))
        keys = jnp.broadcast_to(col_key[t : t + 1, :].astype(F32), (LANES, LANES))
        row_key[place, :] = keys.T.astype(I32)
    own_key[...] = row_key[pl.ds(ROWS * ing, WIDE), :]
    for a in range(ROWS):
        own_wide[8 * a : 8 * (a + 1), :] = jnp.broadcast_to(own_key[a : a + 1, :], (8, LANES))

    def pack_copy(i, slot):
        return pltpu.make_async_remote_copy(
            src_ref=fold.at[:, :, pl.ds(OWN * i, OWN), :], dst_ref=pack_recv.at[:, pl.ds(ROWS * slot, ROWS)],
            send_sem=p_ssem.at[i], recv_sem=p_rsem.at[slot], device_id=on_plane(i, core),
            device_id_type=MESH,
        )

    def fold_rows(h):
        pairs = pair_key[pl.ds(pl.multiple_of(GROUP * h, GROUP), GROUP), :]
        place = pl.ds(pl.multiple_of(GROUP * h, GROUP), GROUP)

        def some_rows(b, carry):
            for a in range(ROWS // 10):
                row = b * (ROWS // 10) + a
                key = own_wide[pl.ds(pl.multiple_of(8 * row, 8), 8), :]
                wanted = (jnp.concatenate([key, key], axis=0) ^ pairs).astype(F32).astype(BF16)
                for which, source in ((0, amp_in), (1, int_in)):
                    folded = jnp.zeros((GROUP, LANES), BF16)
                    for t in range(TILES):
                        part = tile_of(source[h, row], t)
                        folded = jnp.where(wanted == col_half[GROUP * t : GROUP * (t + 1), :], part, folded)
                    fold[which, row, place, :] = folded
            return carry

        lax.fori_loop(0, 10, some_rows, 0)

    own_rows = pltpu.make_async_copy(
        fold.at[:, :, pl.ds(OWN * ing, OWN), :], pack_recv.at[:, pl.ds(ROWS * ing, ROWS)], own_sem.at[0]
    )

    for n, h in enumerate(halves):
        members = [at for at in near if at[0] // 2 == n]
        if n == 0:
            pair_key[pl.ds(OWN * ing, OWN), :] = g_recv[ing]
        for at in members:
            g_copy(ing, peer[at]).wait_recv()
            pair_key[pl.ds(OWN * peer[at], OWN), :] = g_recv[peer[at]]
        for copy in chunk(h):
            copy.wait()
        fold_rows(h)
        for at in members[::-1]:
            pack_copy(peer[at], ing).start()
        if n == 0:
            own_rows.start()
    keys_out = [
        pltpu.make_async_copy(source, target, key_sem.at[n])
        for n, (source, target) in enumerate(
            ((pair_key, pair_key_out), (own_wide, own_wide_out), (col_wide, col_wide_out))
        )
    ]
    for copy in keys_out:
        copy.start()

    fock_rows = fock[...].astype(F32)
    fock_keys = own_key[0:ROWS, :]
    folded_fock = jnp.zeros((ROWS, LANES), F32)
    for t in range(TILES):
        folded_fock = jnp.where(fock_keys == col_key[t : t + 1, :], tile_of(fock_rows, t), folded_fock)
    fock_fold[...] = jnp.zeros(fock_fold.shape, F32)
    fock_fold[0:ROWS, :] = folded_fock
    for t in range(TILES):
        place = slice(LANES * t, LANES * (t + 1))
        row_energy[place, :] = jnp.broadcast_to(col_energy[t : t + 1, :], (LANES, LANES)).T
    for q in range(OWN):
        for t in range(TILES):
            place = slice(LANES * t, LANES * (t + 1))
            wanted = row_key[place, :] ^ pair_irrep[q]
            other = jnp.zeros((LANES, LANES), F32)
            for u in range(TILES):
                other = jnp.where(wanted == col_key[u : u + 1, :], col_energy[u : u + 1, :], other)
            inverse[q, place, :] = 1.0 / (pair_energy[q] - row_energy[place, :] - other)
    lhs[NV:PADDED, :] = jnp.zeros((PADDED - NV, 2 * LANES), BF16)
    int_rhs[NV:PADDED, :] = jnp.zeros((PADDED - NV, 2 * LANES), BF16)
    rhs[:, NV:PADDED, :] = jnp.zeros((OWN, PADDED - NV, 2 * LANES), BF16)

    own_rows.wait()

    for at in near:
        pack_copy(ing, peer[at]).wait_recv()
    for which, target in ((0, lhs), (1, int_rhs)):
        mixed[...] = pack_recv[which].reshape(OWN * NV, LANES).astype(F32)
        for q in range(OWN):
            target[0:NV, LANES * q : LANES * (q + 1)] = mixed[pl.ds(q, NV, stride=OWN), :].astype(BF16)

    for r in range(TILES):
        place = slice(LANES * r, LANES * (r + 1))
        low, high = max(r - 1, 0), min(r + 2, TILES)
        block = lax.dot_general(
            lhs[place, :], int_rhs[LANES * low : LANES * high, :], NT, preferred_element_type=F32
        )
        keys = row_key[place, :]
        folded = jnp.zeros((LANES, LANES), F32)
        for t in range(low, high):
            part = block[:, LANES * (t - low) : LANES * (t - low + 1)]
            folded = jnp.where(keys == col_key[t : t + 1, :], part, folded)
        corr[place, :] = folded

    def red_copy(i, c, slot):
        return pltpu.make_async_remote_copy(
            src_ref=corr.at[pl.ds(ROWS * i + SLICE * c, SLICE)], dst_ref=red_recv.at[slot, pl.ds(0, SLICE)],
            send_sem=r_ssem.at[i * 2 + c], recv_sem=r_rsem.at[slot], device_id=on_plane(i, c),
            device_id_type=MESH,
        )

    for at in far:
        red_copy(peer[at], core, me).start()
        red_copy(peer[at], sibling, me).start()
    red_copy(ing, sibling, me).start()
    red_recv[me, 0:SLICE, :] = corr[pl.ds(ROWS * ing + SLICE * core, SLICE), :]

    for q in range(OWN):
        rhs[q, 0:NV, LANES : 2 * LANES] = -lhs[0:NV, LANES * q : LANES * (q + 1)]

    red_copy(ing, core, ing * 2 + sibling).wait_recv()
    for at in near:
        for c in range(2):
            red_copy(ing, core, peer[at] * 2 + c).wait_recv()
    total = red_recv[0, 0:SLICE, :]
    for w in range(1, PEERS):
        total = total + red_recv[w, 0:SLICE, :]
    z_send[0:SLICE, :] = total

    def z_copy(dest, slot):
        return pltpu.make_async_remote_copy(
            src_ref=z_send.at[pl.ds(0, SLICE)], dst_ref=z_recv.at[slot, pl.ds(0, SLICE)], send_sem=z_ssem.at[dest],
            recv_sem=z_rsem.at[slot], device_id=(dest * 2 + core, ing), device_id_type=MESH,
        )

    for k in above:
        z_copy(above[k], z).start()
    z_recv[z, 0:SLICE, :] = total

    for k in above:
        z_copy(z, above[k]).wait_recv()
    total = z_recv[0, 0:SLICE, :]
    for k in range(1, DEPTH):
        total = total + z_recv[k, 0:SLICE, :]
    op_send[0:SLICE, :] = (fock_fold[pl.ds(SLICE * core, SLICE), :] + total).astype(BF16)

    def op_rows(c):
        return SLICE if c == 0 else ROWS - SLICE

    def op_copy(i, c, source, source_core):
        rows = op_rows(source_core)
        return pltpu.make_async_remote_copy(
            src_ref=op_send.at[pl.ds(0, rows)], dst_ref=op_all.at[pl.ds(ROWS * source + SLICE * source_core, rows)],
            send_sem=o_ssem.at[i * 2 + c], recv_sem=o_rsem.at[source * 2 + source_core],
            device_id=on_plane(i, c), device_id_type=MESH,
        )

    for mine in range(2):

        @pl.when(core == mine)
        def _():
            for at in far:
                for c in range(2):
                    op_copy(peer[at], c, ing, mine).start()
            op_copy(ing, 1 - mine, ing, mine).start()
            own_op = pltpu.make_async_copy(
                op_send.at[pl.ds(0, op_rows(mine))],
                op_all.at[pl.ds(ROWS * ing + SLICE * mine, op_rows(mine))], own_sem.at[1],
            )
            own_op.start()
            own_op.wait()

            op_copy(ing, mine, ing, 1 - mine).wait_recv()

    for at in near:
        for c in range(2):
            op_copy(ing, core, peer[at], c).wait_recv()

    operator = op_all[...]
    for q in range(OWN):
        rhs[q, 0:NV, 0:LANES] = operator
        left = jnp.concatenate([lhs[0:NV, LANES * q : LANES * (q + 1)], operator], axis=1)
        keys = row_key[0:NV, :] ^ pair_irrep[q]
        folded = jnp.zeros((NV, LANES), F32)
        for t in range(0, TILES, 2):
            width = min(2, TILES - t)
            block = lax.dot_general(
                left, rhs[q, LANES * t : LANES * (t + width), :], NT, preferred_element_type=F32
            )
            for u in range(width):
                part = block[:, LANES * u : LANES * (u + 1)]
                folded = jnp.where(keys == col_key[t + u : t + u + 1, :], part, folded)
        mixed[pl.ds(q, NV, stride=OWN), :] = folded * inverse[q, 0:NV, :]
    out_send[...] = mixed[...].astype(BF16).reshape(NV, OWN, LANES)

    def out_copy(i, slot):
        return pltpu.make_async_remote_copy(
            src_ref=out_send.at[pl.ds(ROWS * i, ROWS)], dst_ref=out_recv.at[:, pl.ds(OWN * slot, OWN), :],
            send_sem=t_ssem.at[i], recv_sem=t_rsem.at[slot], device_id=on_plane(i, core),
            device_id_type=MESH,
        )

    for at in far:
        out_copy(peer[at], ing).start()
    own_out = pltpu.make_async_copy(
        out_send.at[pl.ds(ROWS * ing, ROWS)], out_recv.at[:, pl.ds(OWN * ing, OWN), :], own_sem.at[2]
    )
    own_out.start()

    for at in near:
        g_copy(peer[at], ing).wait_send()
        pack_copy(peer[at], ing).wait_send()
        red_copy(peer[at], core, me).wait_send()
        red_copy(peer[at], sibling, me).wait_send()
    red_copy(ing, sibling, me).wait_send()
    for k in above:
        z_copy(above[k], z).wait_send()
    for mine in range(2):

        @pl.when(core == mine)
        def _():
            for at in near:
                for c in range(2):
                    op_copy(peer[at], c, ing, mine).wait_send()
            op_copy(ing, 1 - mine, ing, mine).wait_send()

    for copy in keys_out:
        copy.wait()
    own_out.wait()

    for at in near:
        out_copy(ing, peer[at]).wait_recv()
    for at in near:
        out_copy(peer[at], ing).wait_send()
    result[...] = out_recv[...]


def expand_kernel(folded, pair_key, own_wide, col_wide, update):
    for a in range(update.shape[0]):
        for s in range(GROUP_PAIRS // 8):
            pairs = slice(8 * s, 8 * (s + 1))
            wanted = pair_key[pairs, :] ^ own_wide[8 * a : 8 * (a + 1), :]
            values = folded[a, pairs, :].astype(F32)
            for t in range(TILES):
                width = min(LANES, NV - LANES * t)
                kept = jnp.where(wanted == col_wide[8 * t : 8 * (t + 1), :], values, 0.0)
                update[a, pairs, LANES * t : LANES * t + width] = kept[:, 0:width]


def body(amplitudes, integrals, fock_block, virtual_irrep, pair_irrep, pair_energy, virtual_energy):
    vmem = pl.BlockSpec(memory_space=pltpu.VMEM)
    hbm = pl.BlockSpec(memory_space=pl.ANY)
    dma = pltpu.SemaphoreType.DMA
    result, pair_key, own_wide, col_wide = pl.pallas_call(
        main_kernel,
        name="residual",
        out_shape=(
            jax.ShapeDtypeStruct((ROWS, GROUP_PAIRS, LANES), BF16),
            jax.ShapeDtypeStruct((GROUP_PAIRS, LANES), I32),
            jax.ShapeDtypeStruct((ROWS * 8, LANES), I32),
            jax.ShapeDtypeStruct((TILES * 8, LANES), I32),
        ),
        in_specs=[hbm] * 7,
        out_specs=(vmem, hbm, hbm, hbm),
        scratch_shapes=[
            pltpu.VMEM((ROWS, NV), BF16),
            pltpu.VMEM((NV,), I32),
            pltpu.VMEM((NV,), F32),
            pltpu.SMEM((OWN,), I32),
            pltpu.SMEM((OWN,), F32),
            pltpu.VMEM((ROWS * 8, LANES), I32),
            pltpu.VMEM((TILES * 8, LANES), I32),
            pltpu.VMEM((HALVES, ROWS, GROUP, NV), BF16),
            pltpu.VMEM((HALVES, ROWS, GROUP, NV), BF16),
            pltpu.VMEM((8, LANES), I32),
            pltpu.VMEM((TILES * GROUP, LANES), BF16),
            pltpu.VMEM((8, LANES), F32),
            pltpu.VMEM((PADDED, LANES), I32),
            pltpu.VMEM((PADDED, LANES), F32),
            pltpu.VMEM((WIDE, LANES), I32),
            pltpu.VMEM((GROUP_PAIRS, LANES), I32),
            pltpu.VMEM((OWN, LANES), I32),
            pltpu.VMEM((RING, OWN, LANES), I32),
            pltpu.VMEM((2, ROWS, GROUP_PAIRS, LANES), BF16),
            pltpu.VMEM((2, NV, OWN, LANES), BF16),
            pltpu.VMEM((OWN * NV, LANES), F32),
            pltpu.VMEM((PADDED, 2 * LANES), BF16),
            pltpu.VMEM((OWN, PADDED, 2 * LANES), BF16),
            pltpu.VMEM((PADDED, 2 * LANES), BF16),
            pltpu.VMEM((2 * SLOT, LANES), F32),
            pltpu.VMEM((PADDED, LANES), F32),
            pltpu.VMEM((PEERS, SLOT, LANES), F32),
            pltpu.VMEM((SLOT, LANES), F32),
            pltpu.VMEM((DEPTH, SLOT, LANES), F32),
            pltpu.VMEM((SLOT, LANES), BF16),
            pltpu.VMEM((NV, LANES), BF16),
            pltpu.VMEM((OWN, PADDED, LANES), F32),
            pltpu.VMEM((NV, OWN, LANES), BF16),
            pltpu.VMEM((ROWS, GROUP_PAIRS, LANES), BF16),
            dma((HALVES,)), dma((HALVES,)), dma((RING,)), dma((RING,)), dma((RING,)), dma((RING,)),
            dma((PEERS,)), dma((PEERS,)), dma((DEPTH,)), dma((DEPTH,)), dma((PEERS,)), dma((PEERS,)),
            dma((RING,)), dma((RING,)), dma((3,)), dma((5,)), dma((3,)),
        ],
        compiler_params=pltpu.CompilerParams(collective_id=0, has_side_effects=True),
    )(
        jnp.transpose(amplitudes, (1, 0, 2)), jnp.transpose(integrals, (1, 0, 2)), fock_block,
        virtual_irrep, virtual_energy, pair_irrep, pair_energy,
    )

    step = 25
    update = pl.pallas_call(
        expand_kernel,
        name="expand",
        grid=(ROWS // step,),
        out_shape=jax.ShapeDtypeStruct((ROWS, GROUP_PAIRS, NV), F32),
        in_specs=[
            pl.BlockSpec((step, GROUP_PAIRS, LANES), lambda j: (j, 0, 0)),
            pl.BlockSpec((GROUP_PAIRS, LANES), lambda j: (0, 0)),
            pl.BlockSpec((step * 8, LANES), lambda j: (j, 0)),
            pl.BlockSpec((TILES * 8, LANES), lambda j: (0, 0)),
        ],
        out_specs=pl.BlockSpec((step, GROUP_PAIRS, NV), lambda j: (j, 0, 0)),
    )(result, pair_key, own_wide, col_wide)
    return jnp.transpose(update, (1, 0, 2))


def solution(mesh):
    in_specs = (
        P("grp", "ing", None),
        P("grp", "ing", None),
        P("ing", None),
        P(),
        P(("grp", "ing")),
        P(("grp", "ing")),
        P(),
    )
    out_specs = P("grp", "ing", None)
    return jax.shard_map(body, mesh=mesh, in_specs=in_specs, out_specs=out_specs, check_vma=False)
```

```python
import functools

import jax
import jax.numpy as jnp
from jax import lax
from jax.experimental import pallas as pl
from jax.experimental.pallas import tpu as pltpu
from jax.sharding import PartitionSpec as P

NV, LANES, TILES = 800, 128, 7
PADDED = LANES * TILES
ROWS, OWN, GROUP_PAIRS = 50, 2, 32
GROUP = 16
HALVES = GROUP_PAIRS // GROUP
RING, DEPTH, SIDE = 16, 8, 4
PEERS = 2 * RING
SLICE, SLOT = 26, 32
WIDE = 56
MESH = pl.DeviceIdType.MESH
F32, BF16, I32 = jnp.float32, jnp.bfloat16, jnp.int32
NT = (((1,), (1,)), ((), ()))


def tile_of(array, t):
    if t < TILES - 1:
        return array[:, LANES * t : LANES * (t + 1)]
    last = array[:, LANES * t : NV]
    pad = jnp.zeros((array.shape[0], PADDED - NV), array.dtype)
    return jnp.concatenate([last, pad], axis=1)


def main_kernel(
    amps, ints, fock_in, irrep_in, energy_in, pair_irrep_in, pair_energy_in,
    result, pair_key_out, own_wide_out, col_wide_out,
    fock, irrep, energy, pair_irrep, pair_energy, own_wide, col_wide,
    amp_in, int_in, col_key, col_half, col_energy, row_key, row_energy, own_key, pair_key,
    g_send, g_recv, fold, pack_recv, mixed, lhs, rhs, int_rhs,
    fock_fold, corr, red_recv, z_send, z_recv, op_send, op_all,
    inverse, out_send,
    amp_sem, int_sem, g_ssem, g_rsem, p_ssem, p_rsem, r_ssem, r_rsem,
    z_ssem, z_rsem, o_ssem, o_rsem, t_ssem, t_rsem, own_sem, in_sem, key_sem,
):
    grp, ing = lax.axis_index("grp"), lax.axis_index("ing")
    z, core = grp // 2, grp % 2
    y, x = ing // SIDE, ing % SIDE
    me = ing * 2 + core

    beside = y + 1 - 2 * (y % 2)
    across = [y, beside, (y + 2) % SIDE, (beside + 2) % SIDE]
    along = [(x + k) % SIDE for k in range(SIDE)]
    peer = {(r, k): across[r] * SIDE + along[k] for r in range(SIDE) for k in range(SIDE)}
    hops = {(r, k): (0, 1, 2, 1)[r] + (0, 1, 2, 1)[k] for r in range(SIDE) for k in range(SIDE)}
    near = [at for at in sorted(peer, key=hops.get) if at != (0, 0)]
    far = near[::-1]
    sibling = 1 - core
    above = {k: (z + k) % DEPTH for k in (4, 3, 5, 2, 6, 1, 7)}

    def on_plane(i, c):
        return (z * 2 + c, i)

    def chunk(h):
        place = pl.ds(GROUP * h, GROUP)
        return (
            pltpu.make_async_copy(amps.at[:, place], amp_in.at[h], amp_sem.at[h]),
            pltpu.make_async_copy(ints.at[:, place], int_in.at[h], int_sem.at[h]),
        )

    small = [
        pltpu.make_async_copy(source, target, in_sem.at[n])
        for n, (source, target) in enumerate(
            ((pair_irrep_in, pair_irrep), (irrep_in, irrep), (energy_in, energy),
             (pair_energy_in, pair_energy), (fock_in, fock))
        )
    ]
    for copy in small:
        copy.start()

    barrier = pltpu.get_barrier_semaphore()

    def greet(g, i):
        pl.semaphore_signal(barrier, inc=1, device_id=(g, i), device_id_type=MESH)

    for at in far:
        greet(z * 2 + core, peer[at])
        greet(z * 2 + sibling, peer[at])
    greet(z * 2 + sibling, ing)
    for k in above:
        greet(above[k] * 2 + core, ing)

    halves = [1 - y // 2, y // 2]
    for copy in chunk(halves[0]):
        copy.start()
    small[0].wait()

    for q in range(OWN):
        g_send[q : q + 1, :] = jnp.full((1, LANES), pair_irrep[q], I32)
    g_recv[ing] = g_send[...]

    pl.semaphore_wait(barrier, PEERS - 1 + DEPTH - 1)

    def g_copy(i, slot, c=None):
        return pltpu.make_async_remote_copy(
            src_ref=g_send, dst_ref=g_recv.at[slot], send_sem=g_ssem.at[i], recv_sem=g_rsem.at[slot],
            device_id=on_plane(i, core), device_id_type=MESH,
        )

    for at in far:
        g_copy(peer[at], ing).start()
    for copy in chunk(halves[1]):
        copy.start()
    for copy in small[1:]:
        copy.wait()

    for t in range(TILES):
        if t < TILES - 1:
            col_key[t : t + 1, :] = irrep[LANES * t : LANES * (t + 1)].reshape(1, LANES)
            col_energy[t : t + 1, :] = energy[LANES * t : LANES * (t + 1)].reshape(1, LANES)
        else:
            col_key[t : t + 1, :] = jnp.full((1, LANES), -1, I32)
            col_key[t : t + 1, 0 : NV - LANES * t] = irrep[LANES * t : NV].reshape(1, NV - LANES * t)
            col_energy[t : t + 1, :] = jnp.zeros((1, LANES), F32)
            col_energy[t : t + 1, 0 : NV - LANES * t] = energy[LANES * t : NV].reshape(1, NV - LANES * t)
        col_wide[8 * t : 8 * (t + 1), :] = jnp.broadcast_to(col_key[t : t + 1, :], (8, LANES))
        col_half[GROUP * t : GROUP * (t + 1), :] = jnp.broadcast_to(
            col_key[t : t + 1, :].astype(F32), (GROUP, LANES)
        ).astype(BF16)
    for t in range(TILES):
        place = slice(LANES * t, LANES * (t + 1))
        keys = jnp.broadcast_to(col_key[t : t + 1, :].astype(F32), (LANES, LANES))
        row_key[place, :] = keys.T.astype(I32)
    own_key[...] = row_key[pl.ds(ROWS * ing, WIDE), :]
    for a in range(ROWS):
        own_wide[8 * a : 8 * (a + 1), :] = jnp.broadcast_to(own_key[a : a + 1, :], (8, LANES))

    def pack_copy(i, slot):
        return pltpu.make_async_remote_copy(
            src_ref=fold.at[:, :, pl.ds(OWN * i, OWN), :], dst_ref=pack_recv.at[:, pl.ds(ROWS * slot, ROWS)],
            send_sem=p_ssem.at[i], recv_sem=p_rsem.at[slot], device_id=on_plane(i, core),
            device_id_type=MESH,
        )

    def fold_rows(h):
        pairs = pair_key[pl.ds(pl.multiple_of(GROUP * h, GROUP), GROUP), :]
        place = pl.ds(pl.multiple_of(GROUP * h, GROUP), GROUP)

        def some_rows(b, carry):
            for a in range(ROWS // 10):
                row = b * (ROWS // 10) + a
                key = own_wide[pl.ds(pl.multiple_of(8 * row, 8), 8), :]
                wanted = (jnp.concatenate([key, key], axis=0) ^ pairs).astype(F32).astype(BF16)
                for which, source in ((0, amp_in), (1, int_in)):
                    folded = jnp.zeros((GROUP, LANES), BF16)
                    for t in range(TILES):
                        part = tile_of(source[h, row], t)
                        folded = jnp.where(wanted == col_half[GROUP * t : GROUP * (t + 1), :], part, folded)
                    fold[which, row, place, :] = folded
            return carry

        lax.fori_loop(0, 10, some_rows, 0)

    own_rows = pltpu.make_async_copy(
        fold.at[:, :, pl.ds(OWN * ing, OWN), :], pack_recv.at[:, pl.ds(ROWS * ing, ROWS)], own_sem.at[0]
    )

    for n, h in enumerate(halves):
        members = [at for at in near if at[0] // 2 != n]
        if n == 1:
            pair_key[pl.ds(OWN * ing, OWN), :] = g_recv[ing]
        for at in members:
            g_copy(ing, peer[at]).wait_recv()
            pair_key[pl.ds(OWN * peer[at], OWN), :] = g_recv[peer[at]]
        for copy in chunk(h):
            copy.wait()
        fold_rows(h)
        for at in members[::-1]:
            pack_copy(peer[at], ing).start()
        if n == 1:
            own_rows.start()
    keys_out = [
        pltpu.make_async_copy(source, target, key_sem.at[n])
        for n, (source, target) in enumerate(
            ((pair_key, pair_key_out), (own_wide, own_wide_out), (col_wide, col_wide_out))
        )
    ]
    for copy in keys_out:
        copy.start()

    fock_rows = fock[...].astype(F32)
    fock_keys = own_key[0:ROWS, :]
    folded_fock = jnp.zeros((ROWS, LANES), F32)
    for t in range(TILES):
        folded_fock = jnp.where(fock_keys == col_key[t : t + 1, :], tile_of(fock_rows, t), folded_fock)
    fock_fold[...] = jnp.zeros(fock_fold.shape, F32)
    fock_fold[0:ROWS, :] = folded_fock
    for t in range(TILES):
        place = slice(LANES * t, LANES * (t + 1))
        row_energy[place, :] = jnp.broadcast_to(col_energy[t : t + 1, :], (LANES, LANES)).T
    for q in range(OWN):
        for t in range(TILES):
            place = slice(LANES * t, LANES * (t + 1))
            wanted = row_key[place, :] ^ pair_irrep[q]
            other = jnp.zeros((LANES, LANES), F32)
            for u in range(TILES):
                other = jnp.where(wanted == col_key[u : u + 1, :], col_energy[u : u + 1, :], other)
            inverse[q, place, :] = 1.0 / (pair_energy[q] - row_energy[place, :] - other)
    lhs[NV:PADDED, :] = jnp.zeros((PADDED - NV, 2 * LANES), BF16)
    int_rhs[NV:PADDED, :] = jnp.zeros((PADDED - NV, 2 * LANES), BF16)
    rhs[:, NV:PADDED, :] = jnp.zeros((OWN, PADDED - NV, 2 * LANES), BF16)

    own_rows.wait()

    for at in near:
        pack_copy(ing, peer[at]).wait_recv()
    for which, target in ((0, lhs), (1, int_rhs)):
        mixed[...] = pack_recv[which].reshape(OWN * NV, LANES).astype(F32)
        for q in range(OWN):
            target[0:NV, LANES * q : LANES * (q + 1)] = mixed[pl.ds(q, NV, stride=OWN), :].astype(BF16)

    for r in range(TILES):
        place = slice(LANES * r, LANES * (r + 1))
        low, high = max(r - 1, 0), min(r + 2, TILES)
        block = lax.dot_general(
            lhs[place, :], int_rhs[LANES * low : LANES * high, :], NT, preferred_element_type=F32
        )
        keys = row_key[place, :]
        folded = jnp.zeros((LANES, LANES), F32)
        for t in range(low, high):
            part = block[:, LANES * (t - low) : LANES * (t - low + 1)]
            folded = jnp.where(keys == col_key[t : t + 1, :], part, folded)
        corr[place, :] = folded

    def red_copy(i, c, slot):
        return pltpu.make_async_remote_copy(
            src_ref=corr.at[pl.ds(ROWS * i + SLICE * c, SLICE)], dst_ref=red_recv.at[slot, pl.ds(0, SLICE)],
            send_sem=r_ssem.at[i * 2 + c], recv_sem=r_rsem.at[slot], device_id=on_plane(i, c),
            device_id_type=MESH,
        )

    for at in far:
        red_copy(peer[at], core, me).start()
        red_copy(peer[at], sibling, me).start()
    red_copy(ing, sibling, me).start()
    red_recv[me, 0:SLICE, :] = corr[pl.ds(ROWS * ing + SLICE * core, SLICE), :]

    for q in range(OWN):
        rhs[q, 0:NV, LANES : 2 * LANES] = -lhs[0:NV, LANES * q : LANES * (q + 1)]

    red_copy(ing, core, ing * 2 + sibling).wait_recv()
    for at in near:
        for c in range(2):
            red_copy(ing, core, peer[at] * 2 + c).wait_recv()
    total = red_recv[0, 0:SLICE, :]
    for w in range(1, PEERS):
        total = total + red_recv[w, 0:SLICE, :]
    z_send[0:SLICE, :] = total

    def z_copy(dest, slot):
        return pltpu.make_async_remote_copy(
            src_ref=z_send.at[pl.ds(0, SLICE)], dst_ref=z_recv.at[slot, pl.ds(0, SLICE)], send_sem=z_ssem.at[dest],
            recv_sem=z_rsem.at[slot], device_id=(dest * 2 + core, ing), device_id_type=MESH,
        )

    for k in above:
        z_copy(above[k], z).start()
    z_recv[z, 0:SLICE, :] = total

    for k in above:
        z_copy(z, above[k]).wait_recv()
    total = z_recv[0, 0:SLICE, :]
    for k in range(1, DEPTH):
        total = total + z_recv[k, 0:SLICE, :]
    op_send[0:SLICE, :] = (fock_fold[pl.ds(SLICE * core, SLICE), :] + total).astype(BF16)

    def op_rows(c):
        return SLICE if c == 0 else ROWS - SLICE

    def op_copy(i, c, source, source_core):
        rows = op_rows(source_core)
        return pltpu.make_async_remote_copy(
            src_ref=op_send.at[pl.ds(0, rows)], dst_ref=op_all.at[pl.ds(ROWS * source + SLICE * source_core, rows)],
            send_sem=o_ssem.at[i * 2 + c], recv_sem=o_rsem.at[source * 2 + source_core],
            device_id=on_plane(i, c), device_id_type=MESH,
        )

    for mine in range(2):

        @pl.when(core == mine)
        def _():
            for at in far:
                for c in range(2):
                    op_copy(peer[at], c, ing, mine).start()
            op_copy(ing, 1 - mine, ing, mine).start()
            own_op = pltpu.make_async_copy(
                op_send.at[pl.ds(0, op_rows(mine))],
                op_all.at[pl.ds(ROWS * ing + SLICE * mine, op_rows(mine))], own_sem.at[1],
            )
            own_op.start()
            own_op.wait()

            op_copy(ing, mine, ing, 1 - mine).wait_recv()

    for at in near:
        for c in range(2):
            op_copy(ing, core, peer[at], c).wait_recv()

    operator = op_all[...]
    for q in range(OWN):
        rhs[q, 0:NV, 0:LANES] = operator
        left = jnp.concatenate([lhs[0:NV, LANES * q : LANES * (q + 1)], operator], axis=1)
        keys = row_key[0:NV, :] ^ pair_irrep[q]
        folded = jnp.zeros((NV, LANES), F32)
        for t in range(0, TILES, 2):
            width = min(2, TILES - t)
            block = lax.dot_general(
                left, rhs[q, LANES * t : LANES * (t + width), :], NT, preferred_element_type=F32
            )
            for u in range(width):
                part = block[:, LANES * u : LANES * (u + 1)]
                folded = jnp.where(keys == col_key[t + u : t + u + 1, :], part, folded)
        mixed[pl.ds(q, NV, stride=OWN), :] = folded * inverse[q, 0:NV, :]
    out_send[...] = mixed[...].astype(BF16).reshape(NV, OWN, LANES)

    def out_copy(i, slot):
        return pltpu.make_async_remote_copy(
            src_ref=out_send.at[pl.ds(ROWS * i, ROWS)], dst_ref=result.at[:, pl.ds(OWN * slot, OWN), :],
            send_sem=t_ssem.at[i], recv_sem=t_rsem.at[slot], device_id=on_plane(i, core),
            device_id_type=MESH,
        )

    for at in far:
        out_copy(peer[at], ing).start()
    own_out = pltpu.make_async_copy(
        out_send.at[pl.ds(ROWS * ing, ROWS)], result.at[:, pl.ds(OWN * ing, OWN), :], own_sem.at[2]
    )
    own_out.start()

    for at in near:
        g_copy(peer[at], ing).wait_send()
        pack_copy(peer[at], ing).wait_send()
        red_copy(peer[at], core, me).wait_send()
        red_copy(peer[at], sibling, me).wait_send()
    red_copy(ing, sibling, me).wait_send()
    for k in above:
        z_copy(above[k], z).wait_send()
    for mine in range(2):

        @pl.when(core == mine)
        def _():
            for at in near:
                for c in range(2):
                    op_copy(peer[at], c, ing, mine).wait_send()
            op_copy(ing, 1 - mine, ing, mine).wait_send()

    for copy in keys_out:
        copy.wait()
    own_out.wait()

    for at in near:
        out_copy(ing, peer[at]).wait_recv()
    for at in near:
        out_copy(peer[at], ing).wait_send()


def expand_kernel(folded, pair_key, own_wide, col_wide, update):
    for a in range(update.shape[0]):
        for s in range(GROUP_PAIRS // 8):
            pairs = slice(8 * s, 8 * (s + 1))
            wanted = pair_key[pairs, :] ^ own_wide[8 * a : 8 * (a + 1), :]
            values = folded[a, pairs, :].astype(F32)
            for t in range(TILES):
                width = min(LANES, NV - LANES * t)
                kept = jnp.where(wanted == col_wide[8 * t : 8 * (t + 1), :], values, 0.0)
                update[a, pairs, LANES * t : LANES * t + width] = kept[:, 0:width]


def body(amplitudes, integrals, fock_block, virtual_irrep, pair_irrep, pair_energy, virtual_energy):
    hbm = pl.BlockSpec(memory_space=pl.ANY)
    dma = pltpu.SemaphoreType.DMA
    result, pair_key, own_wide, col_wide = pl.pallas_call(
        main_kernel,
        name="residual",
        out_shape=(
            jax.ShapeDtypeStruct((ROWS, GROUP_PAIRS, LANES), BF16),
            jax.ShapeDtypeStruct((GROUP_PAIRS, LANES), I32),
            jax.ShapeDtypeStruct((ROWS * 8, LANES), I32),
            jax.ShapeDtypeStruct((TILES * 8, LANES), I32),
        ),
        in_specs=[hbm] * 7,
        out_specs=(hbm, hbm, hbm, hbm),
        scratch_shapes=[
            pltpu.VMEM((ROWS, NV), BF16),
            pltpu.VMEM((NV,), I32),
            pltpu.VMEM((NV,), F32),
            pltpu.SMEM((OWN,), I32),
            pltpu.SMEM((OWN,), F32),
            pltpu.VMEM((ROWS * 8, LANES), I32),
            pltpu.VMEM((TILES * 8, LANES), I32),
            pltpu.VMEM((HALVES, ROWS, GROUP, NV), BF16),
            pltpu.VMEM((HALVES, ROWS, GROUP, NV), BF16),
            pltpu.VMEM((8, LANES), I32),
            pltpu.VMEM((TILES * GROUP, LANES), BF16),
            pltpu.VMEM((8, LANES), F32),
            pltpu.VMEM((PADDED, LANES), I32),
            pltpu.VMEM((PADDED, LANES), F32),
            pltpu.VMEM((WIDE, LANES), I32),
            pltpu.VMEM((GROUP_PAIRS, LANES), I32),
            pltpu.VMEM((OWN, LANES), I32),
            pltpu.VMEM((RING, OWN, LANES), I32),
            pltpu.VMEM((2, ROWS, GROUP_PAIRS, LANES), BF16),
            pltpu.VMEM((2, NV, OWN, LANES), BF16),
            pltpu.VMEM((OWN * NV, LANES), F32),
            pltpu.VMEM((PADDED, 2 * LANES), BF16),
            pltpu.VMEM((OWN, PADDED, 2 * LANES), BF16),
            pltpu.VMEM((PADDED, 2 * LANES), BF16),
            pltpu.VMEM((2 * SLOT, LANES), F32),
            pltpu.VMEM((PADDED, LANES), F32),
            pltpu.VMEM((PEERS, SLOT, LANES), F32),
            pltpu.VMEM((SLOT, LANES), F32),
            pltpu.VMEM((DEPTH, SLOT, LANES), F32),
            pltpu.VMEM((SLOT, LANES), BF16),
            pltpu.VMEM((NV, LANES), BF16),
            pltpu.VMEM((OWN, PADDED, LANES), F32),
            pltpu.VMEM((NV, OWN, LANES), BF16),
            dma((HALVES,)), dma((HALVES,)), dma((RING,)), dma((RING,)), dma((RING,)), dma((RING,)),
            dma((PEERS,)), dma((PEERS,)), dma((DEPTH,)), dma((DEPTH,)), dma((PEERS,)), dma((PEERS,)),
            dma((RING,)), dma((RING,)), dma((3,)), dma((5,)), dma((3,)),
        ],
        compiler_params=pltpu.CompilerParams(collective_id=0, has_side_effects=True),
    )(
        jnp.transpose(amplitudes, (1, 0, 2)), jnp.transpose(integrals, (1, 0, 2)), fock_block,
        virtual_irrep, virtual_energy, pair_irrep, pair_energy,
    )

    step = 25
    update = pl.pallas_call(
        expand_kernel,
        name="expand",
        grid=(ROWS // step,),
        out_shape=jax.ShapeDtypeStruct((ROWS, GROUP_PAIRS, NV), F32),
        in_specs=[
            pl.BlockSpec((step, GROUP_PAIRS, LANES), lambda j: (j, 0, 0)),
            pl.BlockSpec((GROUP_PAIRS, LANES), lambda j: (0, 0)),
            pl.BlockSpec((step * 8, LANES), lambda j: (j, 0)),
            pl.BlockSpec((TILES * 8, LANES), lambda j: (0, 0)),
        ],
        out_specs=pl.BlockSpec((step, GROUP_PAIRS, NV), lambda j: (j, 0, 0)),
    )(result, pair_key, own_wide, col_wide)
    return jnp.transpose(update, (1, 0, 2))


def solution(mesh):
    in_specs = (
        P("grp", "ing", None),
        P("grp", "ing", None),
        P("ing", None),
        P(),
        P(("grp", "ing")),
        P(("grp", "ing")),
        P(),
    )
    out_specs = P("grp", "ing", None)
    return jax.shard_map(body, mesh=mesh, in_specs=in_specs, out_specs=out_specs, check_vma=False)
```

```python
import functools

import jax
import jax.numpy as jnp
from jax import lax
from jax.experimental import pallas as pl
from jax.experimental.pallas import tpu as pltpu
from jax.sharding import PartitionSpec as P

NV, LANES, TILES = 800, 128, 7
PADDED = LANES * TILES
ROWS, OWN, GROUP_PAIRS = 50, 2, 32
GROUP = 16
HALVES = GROUP_PAIRS // GROUP
RING, DEPTH, SIDE = 16, 8, 4
PEERS = 2 * RING
SLICE, SLOT = 26, 32
WIDE = 56
MESH = pl.DeviceIdType.MESH
F32, BF16, I32 = jnp.float32, jnp.bfloat16, jnp.int32
NT = (((1,), (1,)), ((), ()))


def tile_of(array, t):
    if t < TILES - 1:
        return array[:, LANES * t : LANES * (t + 1)]
    last = array[:, LANES * t : NV]
    pad = jnp.zeros((array.shape[0], PADDED - NV), array.dtype)
    return jnp.concatenate([last, pad], axis=1)


def main_kernel(
    amps, ints, fock_in, irrep_in, energy_in, pair_irrep_in, pair_energy_in,
    result, pair_key_out, own_wide_out, col_wide_out,
    fock, irrep, energy, pair_irrep, pair_energy, own_wide, col_wide,
    amp_in, int_in, col_key, col_half, col_energy, row_key, row_energy, own_key, pair_key,
    g_send, g_recv, fold, pack_recv, mixed, lhs, rhs, int_rhs,
    fock_fold, corr, red_recv, z_send, z_recv, op_send, op_all,
    inverse, out_send,
    amp_sem, int_sem, g_ssem, g_rsem, p_ssem, p_rsem, r_ssem, r_rsem,
    z_ssem, z_rsem, o_ssem, o_rsem, t_ssem, t_rsem, own_sem, in_sem, key_sem,
):
    grp, ing = lax.axis_index("grp"), lax.axis_index("ing")
    z, core = grp // 2, grp % 2
    y, x = ing // SIDE, ing % SIDE
    me = ing * 2 + core

    beside = y + 1 - 2 * (y % 2)
    across = [y, beside, (y + 2) % SIDE, (beside + 2) % SIDE]
    along = [(x + k) % SIDE for k in range(SIDE)]
    peer = {(r, k): across[r] * SIDE + along[k] for r in range(SIDE) for k in range(SIDE)}
    hops = {(r, k): (0, 1, 2, 1)[r] + (0, 1, 2, 1)[k] for r in range(SIDE) for k in range(SIDE)}
    near = [at for at in sorted(peer, key=hops.get) if at != (0, 0)]
    far = near[::-1]
    sibling = 1 - core
    above = {k: (z + k) % DEPTH for k in (4, 3, 5, 2, 6, 1, 7)}

    def on_plane(i, c):
        return (z * 2 + c, i)

    def chunk(h):
        place = pl.ds(GROUP * h, GROUP)
        return (
            pltpu.make_async_copy(amps.at[:, place], amp_in.at[h], amp_sem.at[h]),
            pltpu.make_async_copy(ints.at[:, place], int_in.at[h], int_sem.at[h]),
        )

    small = [
        pltpu.make_async_copy(source, target, in_sem.at[n])
        for n, (source, target) in enumerate(
            ((pair_irrep_in, pair_irrep), (irrep_in, irrep), (energy_in, energy),
             (pair_energy_in, pair_energy), (fock_in, fock))
        )
    ]
    for copy in small:
        copy.start()

    barrier = pltpu.get_barrier_semaphore()

    def greet(g, i):
        pl.semaphore_signal(barrier, inc=1, device_id=(g, i), device_id_type=MESH)

    for at in far:
        greet(z * 2 + core, peer[at])
        greet(z * 2 + sibling, peer[at])
    greet(z * 2 + sibling, ing)
    for k in above:
        greet(above[k] * 2 + core, ing)

    halves = [1 - y // 2, y // 2]
    for copy in chunk(halves[0]):
        copy.start()
    small[0].wait()

    for q in range(OWN):
        g_send[q : q + 1, :] = jnp.full((1, LANES), pair_irrep[q], I32)
    g_recv[ing] = g_send[...]

    pl.semaphore_wait(barrier, PEERS - 1 + DEPTH - 1)

    def g_copy(i, slot, c=None):
        return pltpu.make_async_remote_copy(
            src_ref=g_send, dst_ref=g_recv.at[slot], send_sem=g_ssem.at[i], recv_sem=g_rsem.at[slot],
            device_id=on_plane(i, core), device_id_type=MESH,
        )

    for at in far:
        g_copy(peer[at], ing).start()
    for copy in chunk(halves[1]):
        copy.start()
    for copy in small[1:]:
        copy.wait()

    for t in range(TILES):
        if t < TILES - 1:
            col_key[t : t + 1, :] = irrep[LANES * t : LANES * (t + 1)].reshape(1, LANES)
            col_energy[t : t + 1, :] = energy[LANES * t : LANES * (t + 1)].reshape(1, LANES)
        else:
            col_key[t : t + 1, :] = jnp.full((1, LANES), -1, I32)
            col_key[t : t + 1, 0 : NV - LANES * t] = irrep[LANES * t : NV].reshape(1, NV - LANES * t)
            col_energy[t : t + 1, :] = jnp.zeros((1, LANES), F32)
            col_energy[t : t + 1, 0 : NV - LANES * t] = energy[LANES * t : NV].reshape(1, NV - LANES * t)
        col_wide[8 * t : 8 * (t + 1), :] = jnp.broadcast_to(col_key[t : t + 1, :], (8, LANES))
        col_half[GROUP * t : GROUP * (t + 1), :] = jnp.broadcast_to(
            col_key[t : t + 1, :].astype(F32), (GROUP, LANES)
        ).astype(BF16)
    for t in range(TILES):
        place = slice(LANES * t, LANES * (t + 1))
        keys = jnp.broadcast_to(col_key[t : t + 1, :].astype(F32), (LANES, LANES))
        row_key[place, :] = keys.T.astype(I32)
    own_key[...] = row_key[pl.ds(ROWS * ing, WIDE), :]
    for a in range(ROWS):
        own_wide[8 * a : 8 * (a + 1), :] = jnp.broadcast_to(own_key[a : a + 1, :], (8, LANES))

    def pack_copy(i, slot):
        return pltpu.make_async_remote_copy(
            src_ref=fold.at[:, :, pl.ds(OWN * i, OWN), :], dst_ref=pack_recv.at[:, pl.ds(ROWS * slot, ROWS)],
            send_sem=p_ssem.at[i], recv_sem=p_rsem.at[slot], device_id=on_plane(i, core),
            device_id_type=MESH,
        )

    def fold_rows(h):
        pairs = pair_key[pl.ds(pl.multiple_of(GROUP * h, GROUP), GROUP), :]
        place = pl.ds(pl.multiple_of(GROUP * h, GROUP), GROUP)

        def some_rows(b, carry):
            for a in range(ROWS // 10):
                row = b * (ROWS // 10) + a
                key = own_wide[pl.ds(pl.multiple_of(8 * row, 8), 8), :]
                wanted = (jnp.concatenate([key, key], axis=0) ^ pairs).astype(F32).astype(BF16)
                for which, source in ((0, amp_in), (1, int_in)):
                    folded = jnp.zeros((GROUP, LANES), BF16)
                    for t in range(TILES):
                        part = tile_of(source[h, row], t)
                        folded = jnp.where(wanted == col_half[GROUP * t : GROUP * (t + 1), :], part, folded)
                    fold[which, row, place, :] = folded
            return carry

        lax.fori_loop(0, 10, some_rows, 0)

    own_rows = pltpu.make_async_copy(
        fold.at[:, :, pl.ds(OWN * ing, OWN), :], pack_recv.at[:, pl.ds(ROWS * ing, ROWS)], own_sem.at[0]
    )

    for n, h in enumerate(halves):
        members = [at for at in near if at[0] // 2 != n]
        if n == 1:
            pair_key[pl.ds(OWN * ing, OWN), :] = g_recv[ing]
        for at in members:
            g_copy(ing, peer[at]).wait_recv()
            pair_key[pl.ds(OWN * peer[at], OWN), :] = g_recv[peer[at]]
        for copy in chunk(h):
            copy.wait()
        fold_rows(h)
    for at in far:
        pack_copy(peer[at], ing).start()
    own_rows.start()
    keys_out = [
        pltpu.make_async_copy(source, target, key_sem.at[n])
        for n, (source, target) in enumerate(
            ((pair_key, pair_key_out), (own_wide, own_wide_out), (col_wide, col_wide_out))
        )
    ]
    for copy in keys_out:
        copy.start()

    fock_rows = fock[...].astype(F32)
    fock_keys = own_key[0:ROWS, :]
    folded_fock = jnp.zeros((ROWS, LANES), F32)
    for t in range(TILES):
        folded_fock = jnp.where(fock_keys == col_key[t : t + 1, :], tile_of(fock_rows, t), folded_fock)
    fock_fold[...] = jnp.zeros(fock_fold.shape, F32)
    fock_fold[0:ROWS, :] = folded_fock
    for t in range(TILES):
        place = slice(LANES * t, LANES * (t + 1))
        row_energy[place, :] = jnp.broadcast_to(col_energy[t : t + 1, :], (LANES, LANES)).T
    for q in range(OWN):
        for t in range(TILES):
            place = slice(LANES * t, LANES * (t + 1))
            wanted = row_key[place, :] ^ pair_irrep[q]
            other = jnp.zeros((LANES, LANES), F32)
            for u in range(TILES):
                other = jnp.where(wanted == col_key[u : u + 1, :], col_energy[u : u + 1, :], other)
            inverse[q, place, :] = 1.0 / (pair_energy[q] - row_energy[place, :] - other)
    lhs[NV:PADDED, :] = jnp.zeros((PADDED - NV, 2 * LANES), BF16)
    int_rhs[NV:PADDED, :] = jnp.zeros((PADDED - NV, 2 * LANES), BF16)
    rhs[:, NV:PADDED, :] = jnp.zeros((OWN, PADDED - NV, 2 * LANES), BF16)

    own_rows.wait()

    for at in near:
        pack_copy(ing, peer[at]).wait_recv()
    for which, target in ((0, lhs), (1, int_rhs)):
        mixed[...] = pack_recv[which].reshape(OWN * NV, LANES).astype(F32)
        for q in range(OWN):
            target[0:NV, LANES * q : LANES * (q + 1)] = mixed[pl.ds(q, NV, stride=OWN), :].astype(BF16)

    for r in range(TILES):
        place = slice(LANES * r, LANES * (r + 1))
        low, high = max(r - 1, 0), min(r + 2, TILES)
        block = lax.dot_general(
            lhs[place, :], int_rhs[LANES * low : LANES * high, :], NT, preferred_element_type=F32
        )
        keys = row_key[place, :]
        folded = jnp.zeros((LANES, LANES), F32)
        for t in range(low, high):
            part = block[:, LANES * (t - low) : LANES * (t - low + 1)]
            folded = jnp.where(keys == col_key[t : t + 1, :], part, folded)
        corr[place, :] = folded

    def red_copy(i, c, slot):
        return pltpu.make_async_remote_copy(
            src_ref=corr.at[pl.ds(ROWS * i + SLICE * c, SLICE)], dst_ref=red_recv.at[slot, pl.ds(0, SLICE)],
            send_sem=r_ssem.at[i * 2 + c], recv_sem=r_rsem.at[slot], device_id=on_plane(i, c),
            device_id_type=MESH,
        )

    for at in far:
        red_copy(peer[at], core, me).start()
        red_copy(peer[at], sibling, me).start()
    red_copy(ing, sibling, me).start()
    red_recv[me, 0:SLICE, :] = corr[pl.ds(ROWS * ing + SLICE * core, SLICE), :]

    for q in range(OWN):
        rhs[q, 0:NV, LANES : 2 * LANES] = -lhs[0:NV, LANES * q : LANES * (q + 1)]

    red_copy(ing, core, ing * 2 + sibling).wait_recv()
    for at in near:
        for c in range(2):
            red_copy(ing, core, peer[at] * 2 + c).wait_recv()
    total = red_recv[0, 0:SLICE, :]
    for w in range(1, PEERS):
        total = total + red_recv[w, 0:SLICE, :]
    z_send[0:SLICE, :] = total

    def z_copy(dest, slot):
        return pltpu.make_async_remote_copy(
            src_ref=z_send.at[pl.ds(0, SLICE)], dst_ref=z_recv.at[slot, pl.ds(0, SLICE)], send_sem=z_ssem.at[dest],
            recv_sem=z_rsem.at[slot], device_id=(dest * 2 + core, ing), device_id_type=MESH,
        )

    for k in above:
        z_copy(above[k], z).start()
    z_recv[z, 0:SLICE, :] = total

    for k in above:
        z_copy(z, above[k]).wait_recv()
    total = z_recv[0, 0:SLICE, :]
    for k in range(1, DEPTH):
        total = total + z_recv[k, 0:SLICE, :]
    op_send[0:SLICE, :] = (fock_fold[pl.ds(SLICE * core, SLICE), :] + total).astype(BF16)

    def op_rows(c):
        return SLICE if c == 0 else ROWS - SLICE

    def op_copy(i, c, source, source_core):
        rows = op_rows(source_core)
        return pltpu.make_async_remote_copy(
            src_ref=op_send.at[pl.ds(0, rows)], dst_ref=op_all.at[pl.ds(ROWS * source + SLICE * source_core, rows)],
            send_sem=o_ssem.at[i * 2 + c], recv_sem=o_rsem.at[source * 2 + source_core],
            device_id=on_plane(i, c), device_id_type=MESH,
        )

    for mine in range(2):

        @pl.when(core == mine)
        def _():
            for at in far:
                for c in range(2):
                    op_copy(peer[at], c, ing, mine).start()
            op_copy(ing, 1 - mine, ing, mine).start()
            own_op = pltpu.make_async_copy(
                op_send.at[pl.ds(0, op_rows(mine))],
                op_all.at[pl.ds(ROWS * ing + SLICE * mine, op_rows(mine))], own_sem.at[1],
            )
            own_op.start()
            own_op.wait()

            op_copy(ing, mine, ing, 1 - mine).wait_recv()

    for at in near:
        for c in range(2):
            op_copy(ing, core, peer[at], c).wait_recv()

    for q in range(OWN):
        rhs[q, 0:NV, 0:LANES] = op_all[...]

    def out_copy(i, slot):
        return pltpu.make_async_remote_copy(
            src_ref=out_send.at[pl.ds(ROWS * i, ROWS)], dst_ref=result.at[:, pl.ds(OWN * slot, OWN), :],
            send_sem=t_ssem.at[i], recv_sem=t_rsem.at[slot], device_id=on_plane(i, core),
            device_id_type=MESH,
        )

    count = NV // HALVES
    for n, h in enumerate(halves):
        place = pl.ds(pl.multiple_of(count * h, count), count)
        for q in range(OWN):
            left = jnp.concatenate([lhs[place, LANES * q : LANES * (q + 1)], op_all[place, :]], axis=1)
            keys = row_key[place, :] ^ pair_irrep[q]
            folded = jnp.zeros((count, LANES), F32)
            for t in range(0, TILES, 2):
                width = min(2, TILES - t)
                block = lax.dot_general(
                    left, rhs[q, LANES * t : LANES * (t + width), :], NT, preferred_element_type=F32
                )
                for u in range(width):
                    part = block[:, LANES * u : LANES * (u + 1)]
                    folded = jnp.where(keys == col_key[t + u : t + u + 1, :], part, folded)
            mixed[pl.ds(q, count, stride=OWN), :] = folded * inverse[q, place, :]
        out_send[place] = mixed[0 : OWN * count, :].astype(BF16).reshape(count, OWN, LANES)
        for at in far:
            if at[0] // 2 != n:
                out_copy(peer[at], ing).start()
    own_out = pltpu.make_async_copy(
        out_send.at[pl.ds(ROWS * ing, ROWS)], result.at[:, pl.ds(OWN * ing, OWN), :], own_sem.at[2]
    )
    own_out.start()

    for at in near:
        g_copy(peer[at], ing).wait_send()
        pack_copy(peer[at], ing).wait_send()
        red_copy(peer[at], core, me).wait_send()
        red_copy(peer[at], sibling, me).wait_send()
    red_copy(ing, sibling, me).wait_send()
    for k in above:
        z_copy(above[k], z).wait_send()
    for mine in range(2):

        @pl.when(core == mine)
        def _():
            for at in near:
                for c in range(2):
                    op_copy(peer[at], c, ing, mine).wait_send()
            op_copy(ing, 1 - mine, ing, mine).wait_send()

    for copy in keys_out:
        copy.wait()
    own_out.wait()

    for at in near:
        out_copy(ing, peer[at]).wait_recv()
    for at in near:
        out_copy(peer[at], ing).wait_send()


def expand_kernel(folded, pair_key, own_wide, col_wide, update):
    for a in range(update.shape[0]):
        for s in range(GROUP_PAIRS // 8):
            pairs = slice(8 * s, 8 * (s + 1))
            wanted = pair_key[pairs, :] ^ own_wide[8 * a : 8 * (a + 1), :]
            values = folded[a, pairs, :].astype(F32)
            for t in range(TILES):
                width = min(LANES, NV - LANES * t)
                kept = jnp.where(wanted == col_wide[8 * t : 8 * (t + 1), :], values, 0.0)
                update[a, pairs, LANES * t : LANES * t + width] = kept[:, 0:width]


def body(amplitudes, integrals, fock_block, virtual_irrep, pair_irrep, pair_energy, virtual_energy):
    hbm = pl.BlockSpec(memory_space=pl.ANY)
    dma = pltpu.SemaphoreType.DMA
    result, pair_key, own_wide, col_wide = pl.pallas_call(
        main_kernel,
        name="residual",
        out_shape=(
            jax.ShapeDtypeStruct((ROWS, GROUP_PAIRS, LANES), BF16),
            jax.ShapeDtypeStruct((GROUP_PAIRS, LANES), I32),
            jax.ShapeDtypeStruct((ROWS * 8, LANES), I32),
            jax.ShapeDtypeStruct((TILES * 8, LANES), I32),
        ),
        in_specs=[hbm] * 7,
        out_specs=(hbm, hbm, hbm, hbm),
        scratch_shapes=[
            pltpu.VMEM((ROWS, NV), BF16),
            pltpu.VMEM((NV,), I32),
            pltpu.VMEM((NV,), F32),
            pltpu.SMEM((OWN,), I32),
            pltpu.SMEM((OWN,), F32),
            pltpu.VMEM((ROWS * 8, LANES), I32),
            pltpu.VMEM((TILES * 8, LANES), I32),
            pltpu.VMEM((HALVES, ROWS, GROUP, NV), BF16),
            pltpu.VMEM((HALVES, ROWS, GROUP, NV), BF16),
            pltpu.VMEM((8, LANES), I32),
            pltpu.VMEM((TILES * GROUP, LANES), BF16),
            pltpu.VMEM((8, LANES), F32),
            pltpu.VMEM((PADDED, LANES), I32),
            pltpu.VMEM((PADDED, LANES), F32),
            pltpu.VMEM((WIDE, LANES), I32),
            pltpu.VMEM((GROUP_PAIRS, LANES), I32),
            pltpu.VMEM((OWN, LANES), I32),
            pltpu.VMEM((RING, OWN, LANES), I32),
            pltpu.VMEM((2, ROWS, GROUP_PAIRS, LANES), BF16),
            pltpu.VMEM((2, NV, OWN, LANES), BF16),
            pltpu.VMEM((OWN * NV, LANES), F32),
            pltpu.VMEM((PADDED, 2 * LANES), BF16),
            pltpu.VMEM((OWN, PADDED, 2 * LANES), BF16),
            pltpu.VMEM((PADDED, 2 * LANES), BF16),
            pltpu.VMEM((2 * SLOT, LANES), F32),
            pltpu.VMEM((PADDED, LANES), F32),
            pltpu.VMEM((PEERS, SLOT, LANES), F32),
            pltpu.VMEM((SLOT, LANES), F32),
            pltpu.VMEM((DEPTH, SLOT, LANES), F32),
            pltpu.VMEM((SLOT, LANES), BF16),
            pltpu.VMEM((NV, LANES), BF16),
            pltpu.VMEM((OWN, PADDED, LANES), F32),
            pltpu.VMEM((NV, OWN, LANES), BF16),
            dma((HALVES,)), dma((HALVES,)), dma((RING,)), dma((RING,)), dma((RING,)), dma((RING,)),
            dma((PEERS,)), dma((PEERS,)), dma((DEPTH,)), dma((DEPTH,)), dma((PEERS,)), dma((PEERS,)),
            dma((RING,)), dma((RING,)), dma((3,)), dma((5,)), dma((3,)),
        ],
        compiler_params=pltpu.CompilerParams(collective_id=0, has_side_effects=True),
    )(
        jnp.transpose(amplitudes, (1, 0, 2)), jnp.transpose(integrals, (1, 0, 2)), fock_block,
        virtual_irrep, virtual_energy, pair_irrep, pair_energy,
    )

    step = 25
    update = pl.pallas_call(
        expand_kernel,
        name="expand",
        grid=(ROWS // step,),
        out_shape=jax.ShapeDtypeStruct((ROWS, GROUP_PAIRS, NV), F32),
        in_specs=[
            pl.BlockSpec((step, GROUP_PAIRS, LANES), lambda j: (j, 0, 0)),
            pl.BlockSpec((GROUP_PAIRS, LANES), lambda j: (0, 0)),
            pl.BlockSpec((step * 8, LANES), lambda j: (j, 0)),
            pl.BlockSpec((TILES * 8, LANES), lambda j: (0, 0)),
        ],
        out_specs=pl.BlockSpec((step, GROUP_PAIRS, NV), lambda j: (j, 0, 0)),
    )(result, pair_key, own_wide, col_wide)
    return jnp.transpose(update, (1, 0, 2))


def solution(mesh):
    in_specs = (
        P("grp", "ing", None),
        P("grp", "ing", None),
        P("ing", None),
        P(),
        P(("grp", "ing")),
        P(("grp", "ing")),
        P(),
    )
    out_specs = P("grp", "ing", None)
    return jax.shard_map(body, mesh=mesh, in_specs=in_specs, out_specs=out_specs, check_vma=False)
```

```python
import functools

import jax
import jax.numpy as jnp
from jax import lax
from jax.experimental import pallas as pl
from jax.experimental.pallas import tpu as pltpu
from jax.sharding import PartitionSpec as P

NV, LANES, TILES = 800, 128, 7
PADDED = LANES * TILES
ROWS, OWN, GROUP_PAIRS = 50, 2, 32
GROUP = 16
HALVES = GROUP_PAIRS // GROUP
RING, DEPTH, SIDE = 16, 8, 4
PEERS = 2 * RING
SLICE, SLOT = 26, 32
WIDE = 56
MESH = pl.DeviceIdType.MESH
F32, BF16, I32 = jnp.float32, jnp.bfloat16, jnp.int32
NT = (((1,), (1,)), ((), ()))


def tile_of(array, t):
    if t < TILES - 1:
        return array[:, LANES * t : LANES * (t + 1)]
    last = array[:, LANES * t : NV]
    pad = jnp.zeros((array.shape[0], PADDED - NV), array.dtype)
    return jnp.concatenate([last, pad], axis=1)


def main_kernel(
    amps, ints, fock_in, irrep_in, energy_in, pair_irrep_in, pair_energy_in,
    result, pair_key_out, own_wide_out, col_wide_out,
    fock, irrep, energy, pair_irrep, pair_energy, own_wide, col_wide,
    amp_in, int_in, col_key, col_half, col_energy, row_key, row_energy, own_key, pair_key,
    g_send, g_recv, fold, pack_recv, mixed, lhs, rhs, int_rhs,
    fock_fold, corr, pair_recv, red_send, red_recv, z_send, z_recv, op_send, op_all,
    inverse, out_send,
    amp_sem, int_sem, g_ssem, g_rsem, p_ssem, p_rsem, s_ssem, s_rsem, r_ssem, r_rsem,
    z_ssem, z_rsem, o_ssem, o_rsem, t_ssem, t_rsem, own_sem, in_sem, key_sem,
):
    grp, ing = lax.axis_index("grp"), lax.axis_index("ing")
    z, core = grp // 2, grp % 2
    y, x = ing // SIDE, ing % SIDE

    beside = y + 1 - 2 * (y % 2)
    across = [y, beside, (y + 2) % SIDE, (beside + 2) % SIDE]
    along = [(x + k) % SIDE for k in range(SIDE)]
    peer = {(r, k): across[r] * SIDE + along[k] for r in range(SIDE) for k in range(SIDE)}
    hops = {(r, k): (0, 1, 2, 1)[r] + (0, 1, 2, 1)[k] for r in range(SIDE) for k in range(SIDE)}
    near = [at for at in sorted(peer, key=hops.get) if at != (0, 0)]
    far = near[::-1]
    sibling = 1 - core
    above = {k: (z + k) % DEPTH for k in (4, 3, 5, 2, 6, 1, 7)}

    def on_plane(i, c):
        return (z * 2 + c, i)

    def chunk(h):
        place = pl.ds(GROUP * h, GROUP)
        return (
            pltpu.make_async_copy(amps.at[:, place], amp_in.at[h], amp_sem.at[h]),
            pltpu.make_async_copy(ints.at[:, place], int_in.at[h], int_sem.at[h]),
        )

    small = [
        pltpu.make_async_copy(source, target, in_sem.at[n])
        for n, (source, target) in enumerate(
            ((pair_irrep_in, pair_irrep), (irrep_in, irrep), (energy_in, energy),
             (pair_energy_in, pair_energy), (fock_in, fock))
        )
    ]
    for copy in small:
        copy.start()

    barrier = pltpu.get_barrier_semaphore()

    def greet(g, i):
        pl.semaphore_signal(barrier, inc=1, device_id=(g, i), device_id_type=MESH)

    for at in far:
        greet(z * 2 + core, peer[at])
        greet(z * 2 + sibling, peer[at])
    greet(z * 2 + sibling, ing)
    for k in above:
        greet(above[k] * 2 + core, ing)

    halves = [1 - y // 2, y // 2]
    for copy in chunk(halves[0]):
        copy.start()
    small[0].wait()

    for q in range(OWN):
        g_send[q : q + 1, :] = jnp.full((1, LANES), pair_irrep[q], I32)
    g_recv[ing] = g_send[...]

    pl.semaphore_wait(barrier, PEERS - 1 + DEPTH - 1)

    def g_copy(i, slot, c=None):
        return pltpu.make_async_remote_copy(
            src_ref=g_send, dst_ref=g_recv.at[slot], send_sem=g_ssem.at[i], recv_sem=g_rsem.at[slot],
            device_id=on_plane(i, core), device_id_type=MESH,
        )

    for at in far:
        g_copy(peer[at], ing).start()
    for copy in chunk(halves[1]):
        copy.start()
    for copy in small[1:]:
        copy.wait()

    for t in range(TILES):
        if t < TILES - 1:
            col_key[t : t + 1, :] = irrep[LANES * t : LANES * (t + 1)].reshape(1, LANES)
            col_energy[t : t + 1, :] = energy[LANES * t : LANES * (t + 1)].reshape(1, LANES)
        else:
            col_key[t : t + 1, :] = jnp.full((1, LANES), -1, I32)
            col_key[t : t + 1, 0 : NV - LANES * t] = irrep[LANES * t : NV].reshape(1, NV - LANES * t)
            col_energy[t : t + 1, :] = jnp.zeros((1, LANES), F32)
            col_energy[t : t + 1, 0 : NV - LANES * t] = energy[LANES * t : NV].reshape(1, NV - LANES * t)
        col_wide[8 * t : 8 * (t + 1), :] = jnp.broadcast_to(col_key[t : t + 1, :], (8, LANES))
        col_half[GROUP * t : GROUP * (t + 1), :] = jnp.broadcast_to(
            col_key[t : t + 1, :].astype(F32), (GROUP, LANES)
        ).astype(BF16)
    for t in range(TILES):
        place = slice(LANES * t, LANES * (t + 1))
        keys = jnp.broadcast_to(col_key[t : t + 1, :].astype(F32), (LANES, LANES))
        row_key[place, :] = keys.T.astype(I32)
    own_key[...] = row_key[pl.ds(ROWS * ing, WIDE), :]
    for a in range(ROWS):
        own_wide[8 * a : 8 * (a + 1), :] = jnp.broadcast_to(own_key[a : a + 1, :], (8, LANES))

    def pack_copy(i, slot):
        return pltpu.make_async_remote_copy(
            src_ref=fold.at[:, :, pl.ds(OWN * i, OWN), :], dst_ref=pack_recv.at[:, pl.ds(ROWS * slot, ROWS)],
            send_sem=p_ssem.at[i], recv_sem=p_rsem.at[slot], device_id=on_plane(i, core),
            device_id_type=MESH,
        )

    def fold_rows(h):
        pairs = pair_key[pl.ds(pl.multiple_of(GROUP * h, GROUP), GROUP), :]
        place = pl.ds(pl.multiple_of(GROUP * h, GROUP), GROUP)

        def some_rows(b, carry):
            for a in range(ROWS // 10):
                row = b * (ROWS // 10) + a
                key = own_wide[pl.ds(pl.multiple_of(8 * row, 8), 8), :]
                wanted = (jnp.concatenate([key, key], axis=0) ^ pairs).astype(F32).astype(BF16)
                for which, source in ((0, amp_in), (1, int_in)):
                    folded = jnp.zeros((GROUP, LANES), BF16)
                    for t in range(TILES):
                        part = tile_of(source[h, row], t)
                        folded = jnp.where(wanted == col_half[GROUP * t : GROUP * (t + 1), :], part, folded)
                    fold[which, row, place, :] = folded
            return carry

        lax.fori_loop(0, 10, some_rows, 0)

    own_rows = pltpu.make_async_copy(
        fold.at[:, :, pl.ds(OWN * ing, OWN), :], pack_recv.at[:, pl.ds(ROWS * ing, ROWS)], own_sem.at[0]
    )

    for n, h in enumerate(halves):
        members = [at for at in near if at[0] // 2 != n]
        if n == 1:
            pair_key[pl.ds(OWN * ing, OWN), :] = g_recv[ing]
        for at in members:
            g_copy(ing, peer[at]).wait_recv()
            pair_key[pl.ds(OWN * peer[at], OWN), :] = g_recv[peer[at]]
        for copy in chunk(h):
            copy.wait()
        fold_rows(h)
    for at in far:
        pack_copy(peer[at], ing).start()
    own_rows.start()
    keys_out = [
        pltpu.make_async_copy(source, target, key_sem.at[n])
        for n, (source, target) in enumerate(
            ((pair_key, pair_key_out), (own_wide, own_wide_out), (col_wide, col_wide_out))
        )
    ]
    for copy in keys_out:
        copy.start()

    fock_rows = fock[...].astype(F32)
    fock_keys = own_key[0:ROWS, :]
    folded_fock = jnp.zeros((ROWS, LANES), F32)
    for t in range(TILES):
        folded_fock = jnp.where(fock_keys == col_key[t : t + 1, :], tile_of(fock_rows, t), folded_fock)
    fock_fold[...] = jnp.zeros(fock_fold.shape, F32)
    fock_fold[0:ROWS, :] = folded_fock
    for t in range(TILES):
        place = slice(LANES * t, LANES * (t + 1))
        row_energy[place, :] = jnp.broadcast_to(col_energy[t : t + 1, :], (LANES, LANES)).T
    for q in range(OWN):
        for t in range(TILES):
            place = slice(LANES * t, LANES * (t + 1))
            wanted = row_key[place, :] ^ pair_irrep[q]
            other = jnp.zeros((LANES, LANES), F32)
            for u in range(TILES):
                other = jnp.where(wanted == col_key[u : u + 1, :], col_energy[u : u + 1, :], other)
            inverse[q, place, :] = 1.0 / (pair_energy[q] - row_energy[place, :] - other)
    lhs[NV:PADDED, :] = jnp.zeros((PADDED - NV, 2 * LANES), BF16)
    int_rhs[NV:PADDED, :] = jnp.zeros((PADDED - NV, 2 * LANES), BF16)
    rhs[:, NV:PADDED, :] = jnp.zeros((OWN, PADDED - NV, 2 * LANES), BF16)

    own_rows.wait()

    for at in near:
        pack_copy(ing, peer[at]).wait_recv()
    for which, target in ((0, lhs), (1, int_rhs)):
        mixed[...] = pack_recv[which].reshape(OWN * NV, LANES).astype(F32)
        for q in range(OWN):
            target[0:NV, LANES * q : LANES * (q + 1)] = mixed[pl.ds(q, NV, stride=OWN), :].astype(BF16)

    for r in range(TILES):
        place = slice(LANES * r, LANES * (r + 1))
        low, high = max(r - 1, 0), min(r + 2, TILES)
        block = lax.dot_general(
            lhs[place, :], int_rhs[LANES * low : LANES * high, :], NT, preferred_element_type=F32
        )
        keys = row_key[place, :]
        folded = jnp.zeros((LANES, LANES), F32)
        for t in range(low, high):
            part = block[:, LANES * (t - low) : LANES * (t - low + 1)]
            folded = jnp.where(keys == col_key[t : t + 1, :], part, folded)
        corr[place, :] = folded

    def pair_copy(i):
        return pltpu.make_async_remote_copy(
            src_ref=corr.at[pl.ds(ROWS * i + SLICE * sibling, SLICE)], dst_ref=pair_recv.at[i, pl.ds(0, SLICE)],
            send_sem=s_ssem.at[i], recv_sem=s_rsem.at[i], device_id=on_plane(ing, sibling),
            device_id_type=MESH,
        )

    def red_copy(i, slot):
        return pltpu.make_async_remote_copy(
            src_ref=red_send.at[i, pl.ds(0, SLICE)], dst_ref=red_recv.at[slot, pl.ds(0, SLICE)],
            send_sem=r_ssem.at[i], recv_sem=r_rsem.at[slot], device_id=on_plane(i, core),
            device_id_type=MESH,
        )

    for at in far + [(0, 0)]:
        pair_copy(peer[at]).start()
    for at in far + [(0, 0)]:
        i = peer[at]
        pair_copy(i).wait_recv()
        both = corr[pl.ds(ROWS * i + SLICE * core, SLICE), :] + pair_recv[i, 0:SLICE, :]
        if at == (0, 0):
            red_recv[i, 0:SLICE, :] = both
        else:
            red_send[i, 0:SLICE, :] = both
            red_copy(i, ing).start()

    for q in range(OWN):
        rhs[q, 0:NV, LANES : 2 * LANES] = -lhs[0:NV, LANES * q : LANES * (q + 1)]

    for at in near:
        red_copy(ing, peer[at]).wait_recv()
    total = red_recv[0, 0:SLICE, :]
    for w in range(1, RING):
        total = total + red_recv[w, 0:SLICE, :]
    z_send[0:SLICE, :] = total

    def z_copy(dest, slot):
        return pltpu.make_async_remote_copy(
            src_ref=z_send.at[pl.ds(0, SLICE)], dst_ref=z_recv.at[slot, pl.ds(0, SLICE)], send_sem=z_ssem.at[dest],
            recv_sem=z_rsem.at[slot], device_id=(dest * 2 + core, ing), device_id_type=MESH,
        )

    for k in above:
        z_copy(above[k], z).start()
    z_recv[z, 0:SLICE, :] = total

    for k in above:
        z_copy(z, above[k]).wait_recv()
    total = z_recv[0, 0:SLICE, :]
    for k in range(1, DEPTH):
        total = total + z_recv[k, 0:SLICE, :]
    op_send[0:SLICE, :] = (fock_fold[pl.ds(SLICE * core, SLICE), :] + total).astype(BF16)

    def op_rows(c):
        return SLICE if c == 0 else ROWS - SLICE

    def op_copy(i, c, source, source_core):
        rows = op_rows(source_core)
        return pltpu.make_async_remote_copy(
            src_ref=op_send.at[pl.ds(0, rows)], dst_ref=op_all.at[pl.ds(ROWS * source + SLICE * source_core, rows)],
            send_sem=o_ssem.at[i * 2 + c], recv_sem=o_rsem.at[source * 2 + source_core],
            device_id=on_plane(i, c), device_id_type=MESH,
        )

    for mine in range(2):

        @pl.when(core == mine)
        def _():
            for at in far:
                for c in range(2):
                    op_copy(peer[at], c, ing, mine).start()
            op_copy(ing, 1 - mine, ing, mine).start()
            own_op = pltpu.make_async_copy(
                op_send.at[pl.ds(0, op_rows(mine))],
                op_all.at[pl.ds(ROWS * ing + SLICE * mine, op_rows(mine))], own_sem.at[1],
            )
            own_op.start()
            own_op.wait()

            op_copy(ing, mine, ing, 1 - mine).wait_recv()

    for at in near:
        for c in range(2):
            op_copy(ing, core, peer[at], c).wait_recv()

    for q in range(OWN):
        rhs[q, 0:NV, 0:LANES] = op_all[...]

    def out_copy(i, slot):
        return pltpu.make_async_remote_copy(
            src_ref=out_send.at[pl.ds(ROWS * i, ROWS)], dst_ref=result.at[:, pl.ds(OWN * slot, OWN), :],
            send_sem=t_ssem.at[i], recv_sem=t_rsem.at[slot], device_id=on_plane(i, core),
            device_id_type=MESH,
        )

    count = NV // HALVES
    for n, h in enumerate(halves):
        place = pl.ds(pl.multiple_of(count * h, count), count)
        for q in range(OWN):
            left = jnp.concatenate([lhs[place, LANES * q : LANES * (q + 1)], op_all[place, :]], axis=1)
            keys = row_key[place, :] ^ pair_irrep[q]
            folded = jnp.zeros((count, LANES), F32)
            for t in range(0, TILES, 2):
                width = min(2, TILES - t)
                block = lax.dot_general(
                    left, rhs[q, LANES * t : LANES * (t + width), :], NT, preferred_element_type=F32
                )
                for u in range(width):
                    part = block[:, LANES * u : LANES * (u + 1)]
                    folded = jnp.where(keys == col_key[t + u : t + u + 1, :], part, folded)
            mixed[pl.ds(q, count, stride=OWN), :] = folded * inverse[q, place, :]
        out_send[place] = mixed[0 : OWN * count, :].astype(BF16).reshape(count, OWN, LANES)
        for at in far:
            if at[0] // 2 != n:
                out_copy(peer[at], ing).start()
    own_out = pltpu.make_async_copy(
        out_send.at[pl.ds(ROWS * ing, ROWS)], result.at[:, pl.ds(OWN * ing, OWN), :], own_sem.at[2]
    )
    own_out.start()

    for at in near:
        g_copy(peer[at], ing).wait_send()
        pack_copy(peer[at], ing).wait_send()
        red_copy(peer[at], ing).wait_send()
    for at in peer:
        pair_copy(peer[at]).wait_send()
    for k in above:
        z_copy(above[k], z).wait_send()
    for mine in range(2):

        @pl.when(core == mine)
        def _():
            for at in near:
                for c in range(2):
                    op_copy(peer[at], c, ing, mine).wait_send()
            op_copy(ing, 1 - mine, ing, mine).wait_send()

    for copy in keys_out:
        copy.wait()
    own_out.wait()

    for at in near:
        out_copy(ing, peer[at]).wait_recv()
    for at in near:
        out_copy(peer[at], ing).wait_send()


def expand_kernel(folded, pair_key, own_wide, col_wide, update):
    for a in range(update.shape[0]):
        for s in range(GROUP_PAIRS // 8):
            pairs = slice(8 * s, 8 * (s + 1))
            wanted = pair_key[pairs, :] ^ own_wide[8 * a : 8 * (a + 1), :]
            values = folded[a, pairs, :].astype(F32)
            for t in range(TILES):
                width = min(LANES, NV - LANES * t)
                kept = jnp.where(wanted == col_wide[8 * t : 8 * (t + 1), :], values, 0.0)
                update[a, pairs, LANES * t : LANES * t + width] = kept[:, 0:width]


def body(amplitudes, integrals, fock_block, virtual_irrep, pair_irrep, pair_energy, virtual_energy):
    hbm = pl.BlockSpec(memory_space=pl.ANY)
    dma = pltpu.SemaphoreType.DMA
    result, pair_key, own_wide, col_wide = pl.pallas_call(
        main_kernel,
        name="residual",
        out_shape=(
            jax.ShapeDtypeStruct((ROWS, GROUP_PAIRS, LANES), BF16),
            jax.ShapeDtypeStruct((GROUP_PAIRS, LANES), I32),
            jax.ShapeDtypeStruct((ROWS * 8, LANES), I32),
            jax.ShapeDtypeStruct((TILES * 8, LANES), I32),
        ),
        in_specs=[hbm] * 7,
        out_specs=(hbm, hbm, hbm, hbm),
        scratch_shapes=[
            pltpu.VMEM((ROWS, NV), BF16),
            pltpu.VMEM((NV,), I32),
            pltpu.VMEM((NV,), F32),
            pltpu.SMEM((OWN,), I32),
            pltpu.SMEM((OWN,), F32),
            pltpu.VMEM((ROWS * 8, LANES), I32),
            pltpu.VMEM((TILES * 8, LANES), I32),
            pltpu.VMEM((HALVES, ROWS, GROUP, NV), BF16),
            pltpu.VMEM((HALVES, ROWS, GROUP, NV), BF16),
            pltpu.VMEM((8, LANES), I32),
            pltpu.VMEM((TILES * GROUP, LANES), BF16),
            pltpu.VMEM((8, LANES), F32),
            pltpu.VMEM((PADDED, LANES), I32),
            pltpu.VMEM((PADDED, LANES), F32),
            pltpu.VMEM((WIDE, LANES), I32),
            pltpu.VMEM((GROUP_PAIRS, LANES), I32),
            pltpu.VMEM((OWN, LANES), I32),
            pltpu.VMEM((RING, OWN, LANES), I32),
            pltpu.VMEM((2, ROWS, GROUP_PAIRS, LANES), BF16),
            pltpu.VMEM((2, NV, OWN, LANES), BF16),
            pltpu.VMEM((OWN * NV, LANES), F32),
            pltpu.VMEM((PADDED, 2 * LANES), BF16),
            pltpu.VMEM((OWN, PADDED, 2 * LANES), BF16),
            pltpu.VMEM((PADDED, 2 * LANES), BF16),
            pltpu.VMEM((2 * SLOT, LANES), F32),
            pltpu.VMEM((PADDED, LANES), F32),
            pltpu.VMEM((RING, SLOT, LANES), F32),
            pltpu.VMEM((RING, SLOT, LANES), F32),
            pltpu.VMEM((RING, SLOT, LANES), F32),
            pltpu.VMEM((SLOT, LANES), F32),
            pltpu.VMEM((DEPTH, SLOT, LANES), F32),
            pltpu.VMEM((SLOT, LANES), BF16),
            pltpu.VMEM((NV, LANES), BF16),
            pltpu.VMEM((OWN, PADDED, LANES), F32),
            pltpu.VMEM((NV, OWN, LANES), BF16),
            dma((HALVES,)), dma((HALVES,)), dma((RING,)), dma((RING,)), dma((RING,)), dma((RING,)),
            dma((RING,)), dma((RING,)), dma((RING,)), dma((RING,)), dma((DEPTH,)), dma((DEPTH,)), dma((PEERS,)), dma((PEERS,)),
            dma((RING,)), dma((RING,)), dma((3,)), dma((5,)), dma((3,)),
        ],
        compiler_params=pltpu.CompilerParams(collective_id=0, has_side_effects=True),
    )(
        jnp.transpose(amplitudes, (1, 0, 2)), jnp.transpose(integrals, (1, 0, 2)), fock_block,
        virtual_irrep, virtual_energy, pair_irrep, pair_energy,
    )

    step = 25
    update = pl.pallas_call(
        expand_kernel,
        name="expand",
        grid=(ROWS // step,),
        out_shape=jax.ShapeDtypeStruct((ROWS, GROUP_PAIRS, NV), F32),
        in_specs=[
            pl.BlockSpec((step, GROUP_PAIRS, LANES), lambda j: (j, 0, 0)),
            pl.BlockSpec((GROUP_PAIRS, LANES), lambda j: (0, 0)),
            pl.BlockSpec((step * 8, LANES), lambda j: (j, 0)),
            pl.BlockSpec((TILES * 8, LANES), lambda j: (0, 0)),
        ],
        out_specs=pl.BlockSpec((step, GROUP_PAIRS, NV), lambda j: (j, 0, 0)),
    )(result, pair_key, own_wide, col_wide)
    return jnp.transpose(update, (1, 0, 2))


def solution(mesh):
    in_specs = (
        P("grp", "ing", None),
        P("grp", "ing", None),
        P("ing", None),
        P(),
        P(("grp", "ing")),
        P(("grp", "ing")),
        P(),
    )
    out_specs = P("grp", "ing", None)
    return jax.shard_map(body, mesh=mesh, in_specs=in_specs, out_specs=out_specs, check_vma=False)
```
